768 devices in a mesh: rep: 8 (over y_lo, x), fsdp: 96 (over z, y_hi, core).
Axes of the slice: x: 4, y: 8 (y_hi: 4, y_lo: 2; y = y_hi * 2 + y_lo), z: 12, core: 2. Of those that a mesh axis runs over, the one named last changes fastest.
Arguments:
- block_input: bfloat16 [98304, 4096], P(('rep', 'fsdp')), may hold values from -6 to 6
- ssd_input: bfloat16 [98304, 4096], P(('rep', 'fsdp')), may hold values from -6 to 6
- out_grad: bfloat16 [98304, 4096], P(('rep', 'fsdp')), may hold values from -0.29882812 to 0.29882812
- start_state: bfloat16 [768, 64, 4096], P(('rep', 'fsdp')), may hold values from -12 to 12
- step_bias: float32 [64], replicated, may hold values from -1 to 1
- decay_log: float32 [64], replicated, may hold values from -7 to -2.5
- local_params: float32 [8, 192, 4096], P('rep', 'fsdp'), may hold values from -0.09375 to 0.09375
- global_params: float32 [192, 4096], P('fsdp'), may hold values from -0.75 to 0.75
- momentum: float32 [192, 4096], P('fsdp'), may hold values from -3 to 3
Outputs:
- block_grad: bfloat16 [98304, 4096], P(('rep', 'fsdp'))
- new_params: float32 [192, 4096], P('fsdp')
- new_momentum: float32 [192, 4096], P('fsdp')
The draws below stay inside these ranges and needn't reach their ends.
All inputs are finite; a program needn't handle non-finite values.
Results may differ from the reference program's by a relative error of at most 0.012.
Values may be sent and summed in bfloat16 or wider, within the bound.
A program may use at most 32 MiB of HBM per device.

```python
import jax
import jax.numpy as jnp
from jax import lax

D = 4096
HEADS = 64
HEAD_DIM = 64
STATE = 64
BLOCK = 128
COLS = 192
REPLICAS = 8
SEQS = 768
TOKENS = 98304


def shard_levels(rng, dims, shards, least, top_value):
    def one(axis_at, blocks):
        draws = jax.random.uniform(jax.random.fold_in(jax.random.fold_in(rng, 6), axis_at), (blocks,), jnp.float32, least / len(shards), top_value / len(shards))
        return jnp.repeat(jnp.exp(draws), dims[axis_at] // blocks).reshape((-1,) + (1,) * (len(dims) - axis_at - 1))

    loudness = one(*shards[0])
    for cut in shards[1:]:
        loudness = loudness * one(*cut)
    return loudness


def scatter_about(own_key, shape, deviation, limit, split=(), kind=jnp.bfloat16):
    values = deviation * jax.random.normal(own_key, shape, jnp.float32)
    if split:
        values = values * shard_levels(own_key, shape, split, -0.22, 0.18)
    return jnp.clip(values, -limit, limit).astype(kind)


def setup_inputs(seed: int = 0) -> dict:
    splits = jax.random.split(jax.random.key(seed), 10)
    block_input = scatter_about(splits[0], (TOKENS, D), 1.0, 6.0, ((0, 768),))
    ssd_input = scatter_about(splits[1], (TOKENS, HEADS * HEAD_DIM), 1.0, 6.0, ((0, 768),))
    out_grad = scatter_about(splits[2], (TOKENS, HEADS * HEAD_DIM), 0.05, 0.29882812, ((0, 768),))
    start_state = scatter_about(splits[3], (SEQS, HEADS, HEAD_DIM * STATE), 2.0, 12.0, ((0, 768),))
    step_bias = jnp.clip(jax.random.uniform(splits[4], (HEADS,), jnp.float32, -1.0, 1.0), -1.0, 1.0)
    decay_log = jnp.clip(jax.random.uniform(splits[5], (HEADS,), jnp.float32, -7.0, -2.5), -7.0, -2.5)
    local_params = scatter_about(splits[6], (REPLICAS, COLS, D), D ** -0.5, 0.09375, ((0, 8), (1, 96)), jnp.float32)
    global_params = scatter_about(splits[7], (COLS, D), (D // 64) ** -0.5, 0.75, ((0, 96),), jnp.float32)
    momentum = scatter_about(splits[8], (COLS, D), 0.5, 3.0, ((0, 96),), jnp.float32)
    return dict(block_input=block_input, ssd_input=ssd_input, out_grad=out_grad, start_state=start_state, step_bias=step_bias, decay_log=decay_log, local_params=local_params, global_params=global_params, momentum=momentum)


inner_rate = 0.002
outer_rate = 0.7
momentum_decay = 0.9

def contract_last(left, right):
    return lax.dot_general(left, right, (((1,), (1,)), ((), ())), preferred_element_type=jnp.float32)

def ssd_forward(projected, values, carried_in, step_bias, decay_log):
    key_side = projected[:, :STATE]
    query_side = projected[:, STATE:2 * STATE]
    step_size = jax.nn.softplus(projected[:, 2 * STATE:] + step_bias)
    cumulative = jnp.cumsum(-step_size * jnp.exp(decay_log), axis=0)
    positions = jnp.arange(BLOCK)
    causal = positions[:, None] >= positions[None, :]
    spans = cumulative.T[:, :, None] - cumulative.T[:, None, :]
    decays = jnp.where(causal, jnp.exp(jnp.where(causal, spans, 0.0)), 0.0)
    scores = jnp.dot(query_side, key_side.T, precision=lax.Precision.HIGHEST)
    mixing = scores[None] * decays
    scaled = values.astype(jnp.float32).reshape(BLOCK, HEADS, HEAD_DIM) * step_size[:, :, None]
    within = jnp.einsum('hts,shp->thp', mixing, scaled, precision=lax.Precision.HIGHEST)
    state_f = carried_in.astype(jnp.float32).reshape(HEADS, HEAD_DIM, STATE)
    entering = jnp.einsum('tn,hpn->thp', query_side, state_f, precision=lax.Precision.HIGHEST)
    entering = entering * jnp.exp(cumulative)[:, :, None]
    return (within + entering).reshape(BLOCK, HEADS * HEAD_DIM)

def sequence_grads(projected, ssd_rows, cot_rows, states, step_bias, decay_log):
    blocks = projected.shape[0] // BLOCK

    def single(members):
        proj_one, values, cotangent, carried_in = members
        _, pullback = jax.vjp(lambda probe: ssd_forward(probe, values, carried_in, step_bias, decay_log), proj_one)
        return pullback(cotangent.astype(jnp.float32))[0]
    grads = lax.map(single, (projected.reshape(blocks, BLOCK, -1), ssd_rows.reshape(blocks, BLOCK, -1), cot_rows.reshape(blocks, BLOCK, -1), states))
    return grads.reshape(blocks * BLOCK, -1)

def reference(block_input, ssd_input, out_grad, start_state, step_bias, decay_log, local_params, global_params, momentum):
    replicas = local_params.shape[0]

    def replica(members):
        rows_in, ssd_rows, cot_rows, states, params = members
        weights = params.astype(jnp.bfloat16)
        projected = contract_last(rows_in, weights)
        proj_grad = sequence_grads(projected, ssd_rows, cot_rows, states, step_bias, decay_log).astype(jnp.bfloat16)
        block_grad = jnp.dot(proj_grad, weights, preferred_element_type=jnp.float32).astype(jnp.bfloat16)
        gradient = jnp.dot(proj_grad.T, rows_in, preferred_element_type=jnp.float32)
        return (block_grad, params - inner_rate * gradient)
    stacked = (block_input.reshape(replicas, -1, D), ssd_input.reshape(replicas, -1, HEADS * HEAD_DIM), out_grad.reshape(replicas, -1, HEADS * HEAD_DIM), start_state.reshape(replicas, -1, HEADS, HEAD_DIM * STATE), local_params)
    block_grad, stepped = lax.map(replica, stacked)
    pseudo = global_params[None] - stepped
    mean_pseudo = lax.optimization_barrier(jnp.sum(pseudo, axis=0)) / replicas
    new_momentum = momentum_decay * momentum + mean_pseudo
    new_params = global_params - outer_rate * (mean_pseudo + momentum_decay * new_momentum)
    return (block_grad.reshape(-1, D), new_params, new_momentum)
```

```python
import jax
import jax.numpy as jnp
from jax import lax
from jax.experimental import pallas as pl
from jax.experimental.pallas import tpu as pltpu
from jax.sharding import PartitionSpec as P

HEADS = 64
STATE = 64
BLOCK = 128
D = 4096
COLS = 192
NX, NYL, NYH, NZ, NC = 4, 2, 4, 12, 2
SLICE = D // (NX * NC)
HALF = D // NC
CHUNKS = 4
CHUNK = HALF // CHUNKS
RIGHT, LEFT = 6, 5

inner_rate = 0.002
outer_rate = 0.7
momentum_decay = 0.9

MESH = pl.DeviceIdType.MESH
F32 = jnp.float32
BF16 = jnp.bfloat16
EXACT = lax.Precision.HIGHEST


def place():
    rep = lax.axis_index("rep")
    fsdp = lax.axis_index("fsdp")
    x = lax.rem(rep, NX)
    yl = lax.div(rep, NX)
    z = lax.div(fsdp, NYH * NC)
    yh = lax.rem(lax.div(fsdp, NC), NYH)
    c = lax.rem(fsdp, NC)
    return x, yl, yh, z, c


def device(x, yl, yh, z, c):
    return (yl * NX + x, z * (NYH * NC) + yh * NC + c)


def shift(i, by, n):
    return lax.rem(i + by, n)


def greet(devices):
    barrier = pltpu.get_barrier_semaphore()
    for target in devices:
        pl.semaphore_signal(barrier, inc=1, device_id=target, device_id_type=MESH)
    pl.semaphore_wait(barrier, len(devices))


def replica_group(x, yl, yh, z, c):
    return [
        device(shift(x, dx, NX), shift(yl, dy, NYL), yh, z, shift(c, dc, NC))
        for dx in range(NX)
        for dy in range(NYL)
        for dc in range(NC)
        if (dx, dy, dc) != (0, 0, 0)
    ]


def remote(src, dst, send_sem, recv_sem, target):
    return pltpu.make_async_remote_copy(
        src_ref=src,
        dst_ref=dst,
        send_sem=send_sem,
        recv_sem=recv_sem,
        device_id=target,
        device_id_type=MESH,
    )


def wait_bytes(ref, sem):
    pltpu.make_async_copy(ref, ref, sem).wait()


def gather_kernel(
    rows_ref, input_ref, w_ref, cols_ref, params_ref,
    shards, block32, sem_send, sem_recv, ring_right, ring_left, sem_self,
):
    x, yl, yh, z, c = place()
    me_a = yh * NC + c
    me_q = x * NC + c
    me_r = yl * NX + x
    local = [
        device(x, yl, shift(yh, dy, NYH), z, shift(c, dc, NC))
        for dy in range(NYH)
        for dc in range(NC)
        if (dy, dc) != (0, 0)
    ]
    right = device(x, yl, yh, shift(z, 1, NZ), c)
    left = device(x, yl, yh, shift(z, NZ - 1, NZ), c)
    partner = device(x, yl, yh, z, 1 - c)
    greet(local + [right, left] + replica_group(x, yl, yh, z, c))

    def half(core):
        return pl.ds(pl.multiple_of(core * HALF, HALF), HALF)

    def part(q):
        return pl.ds(pl.multiple_of(q * SLICE, SLICE), SLICE)

    for dy in (2, 1, 3, 0):
        for dc in range(NC):
            core = shift(c, dc, NC)
            src = rows_ref.at[0, :, half(core)]
            dst = shards.at[me_a]
            if (dy, dc) == (0, 0):
                pltpu.make_async_copy(src, dst, sem_recv.at[0]).start()
            else:
                remote(
                    src, dst, sem_send.at[0], sem_recv.at[0],
                    device(x, yl, shift(yh, dy, NYH), z, core),
                ).start()
    for dx in (2, 1, 3, 0):
        for dc in range(NC):
            tx, core = shift(x, dx, NX), shift(c, dc, NC)
            src = input_ref.at[:, part(tx * NC + core)]
            dst = cols_ref.at[me_q]
            if (dx, dc) == (0, 0):
                pltpu.make_async_copy(src, dst, sem_recv.at[1]).start()
            else:
                remote(
                    src, dst, sem_send.at[1], sem_recv.at[1], device(tx, yl, yh, z, core)
                ).start()
    own = yl == c
    for dx in (2, 1, 3, 0):
        for dc in range(NC):
            tx, core = shift(x, dx, NX), shift(c, dc, NC)
            src = rows_ref.at[0, :, part(tx * NC + core)]
            dst = params_ref.at[me_r]
            if (dx, dc) == (0, 0):
                pl.when(own)(pltpu.make_async_copy(src, dst, sem_recv.at[2]).start)
                copy = remote(
                    src, dst, sem_self, sem_recv.at[2], device(tx, 1 - yl, yh, z, core)
                )
                pl.when(jnp.logical_not(own))(copy.start)
            else:
                remote(
                    src, dst, sem_send.at[2], sem_recv.at[2], device(tx, c, yh, z, core)
                ).start()

    wait_bytes(shards, sem_recv.at[0])
    for i in range(NYH * NC):
        block32[2 * i : 2 * i + 2, :] = shards[i]
    w_ref[z, :, half(c)] = block32[...].astype(BF16)

    def chunk(b, k):
        return w_ref.at[b, :, pl.ds(pl.multiple_of(c * HALF + k * CHUNK, CHUNK), CHUNK)]

    def pass_on(b):
        block = w_ref.at[b, :, half(c)]
        remote(block, block, sem_send.at[4], sem_recv.at[3], partner).start()

    for s in range(RIGHT + 1):
        br = shift(z, NZ - s, NZ)
        bl = shift(z, s, NZ)
        for k in range(CHUNKS):
            if s > 0:
                remote(
                    chunk(br, k), chunk(br, k), sem_send.at[3], ring_right.at[s - 1, k], right
                ).wait_recv()
            if s < RIGHT:
                remote(
                    chunk(br, k), chunk(br, k), sem_send.at[3], ring_right.at[s, k], right
                ).start()
            if 0 < s <= LEFT:
                remote(
                    chunk(bl, k), chunk(bl, k), sem_send.at[3], ring_left.at[s - 1, k], left
                ).wait_recv()
            if s < LEFT:
                remote(
                    chunk(bl, k), chunk(bl, k), sem_send.at[3], ring_left.at[s, k], left
                ).start()
        pass_on(br)
        if 0 < s <= LEFT:
            pass_on(bl)

    wait_bytes(cols_ref, sem_recv.at[1])
    wait_bytes(params_ref, sem_recv.at[2])
    wait_bytes(w_ref.at[:, :, half(1 - c)], sem_recv.at[3])
    wait_bytes(shards.at[0:7], sem_send.at[0])
    wait_bytes(cols_ref.at[0:7], sem_send.at[1])
    wait_bytes(params_ref.at[0:7], sem_send.at[2])
    wait_bytes(w_ref.at[0 : RIGHT + LEFT, :, half(c)], sem_send.at[3])
    wait_bytes(w_ref.at[:, :, half(c)], sem_send.at[4])

    @pl.when(jnp.logical_not(own))
    def _():
        wait_bytes(params_ref.at[0], sem_self)


def gather(rows, block_input):
    vmem = pl.BlockSpec(memory_space=pltpu.VMEM)
    hbm = pl.BlockSpec(memory_space=pl.ANY)
    return pl.pallas_call(
        gather_kernel,
        out_shape=(
            jax.ShapeDtypeStruct((NZ, COLS // NZ, D), BF16),
            jax.ShapeDtypeStruct((NX * NC, BLOCK, SLICE), BF16),
            jax.ShapeDtypeStruct((NX * NYL, 2, SLICE), F32),
        ),
        in_specs=[hbm, hbm],
        out_specs=(vmem, vmem, vmem),
        scratch_shapes=[
            pltpu.VMEM((NYH * NC, 2, HALF), F32),
            pltpu.VMEM((COLS // NZ, HALF), F32),
            pltpu.SemaphoreType.DMA((5,)),
            pltpu.SemaphoreType.DMA((4,)),
            pltpu.SemaphoreType.DMA((RIGHT, CHUNKS)),
            pltpu.SemaphoreType.DMA((LEFT, CHUNKS)),
            pltpu.SemaphoreType.DMA,
        ],
        compiler_params=pltpu.CompilerParams(collective_id=0, has_side_effects=True),
        name="gather_rows",
    )(rows, block_input)


def dot(a, b, dims, precision=None):
    return lax.dot_general(
        a, b, ((dims[0], dims[1]), ((), ())), precision=precision, preferred_element_type=F32
    )


NN = ((1,), (0,))
NT = ((1,), (1,))
TN = ((0,), (0,))
GROUP = 8


def block_kernel(
    x_ref, values_ref, cot_ref, state_ref, bias_ref, decay_ref, w_ref,
    out_ref, grad_ref,
    cum_groups, row_groups, both_t, col_t, ds_ref, dq_ref,
):
    proj = dot(x_ref[...], w_ref[...], NT)
    key = proj[:, :STATE]
    query = proj[:, STATE : 2 * STATE]
    raw = proj[:, 2 * STATE :] + bias_ref[...]
    rate = jnp.exp(decay_ref[...])
    step = jnp.maximum(raw, 0.0) + jnp.log1p(jnp.exp(-jnp.abs(raw)))
    t_index = lax.broadcasted_iota(jnp.int32, (BLOCK, BLOCK), 0)
    s_index = lax.broadcasted_iota(jnp.int32, (BLOCK, BLOCK), 1)
    causal = t_index >= s_index
    lower = jnp.where(causal, 1.0, 0.0)
    upper = jnp.where(t_index <= s_index, 1.0, 0.0)
    cum = dot(lower, -step * rate, NN, EXACT)
    both_t[...] = jnp.concatenate([cum, step], axis=1).T
    wide = jnp.concatenate([cum, step], axis=1)
    for g in range(HEADS // GROUP):
        cum_groups[g] = pltpu.roll(wide, (BLOCK - GROUP * g) % BLOCK, 1) if g else wide
    scores = jnp.where(causal, dot(query, key, NT, EXACT), 0.0)
    query_twice = jnp.concatenate([query, query], axis=1)
    ds_ref[...] = jnp.zeros_like(ds_ref)
    dq_ref[...] = jnp.zeros_like(dq_ref)
    first = s_index < STATE
    first16 = lax.broadcasted_iota(jnp.int32, (BLOCK, BLOCK), 1) < STATE
    column = lax.rem(s_index, STATE)
    origin = (s_index - column) + 2 * lax.rem(column, STATE // 2) + lax.div(column, STATE // 2)
    order = jnp.where(t_index == origin, 1.0, 0.0).astype(BF16)
    low = lax.broadcasted_iota(jnp.int32, (STATE // 2, BLOCK), 1) < STATE
    zero_state = jnp.zeros((STATE // 2, BLOCK), BF16)

    @pl.loop(0, HEADS // GROUP)
    def _(g):
        cum_g = cum_groups[g]
        at = pl.multiple_of(g * GROUP, GROUP)
        cum_rows = both_t[pl.ds(at, GROUP), :]
        step_rows = both_t[pl.ds(HEADS + at, GROUP), :]
        rows = jnp.zeros((BLOCK, BLOCK), F32)
        cols = []
        for j in range(GROUP // 2):
            lanes = pl.ds(pl.multiple_of(g * (GROUP * STATE) + j * BLOCK, BLOCK), BLOCK)
            cot = cot_ref[:, lanes]
            val = values_ref[:, lanes]
            zero = jnp.zeros_like(val)
            pair = jnp.concatenate(
                [jnp.where(first16, val, zero), jnp.where(first16, zero, val)], axis=0
            )
            inner = dot(cot, pair, NT)
            sorted_cot = dot(cot, order, NN).astype(BF16)
            states = []
            for e in range(2):
                st = state_ref[g * GROUP + 2 * j + e]
                own = [jnp.where(low, st, zero_state), jnp.where(low, zero_state, st)]
                rest = [zero_state, zero_state]
                states.append(jnp.concatenate(own + rest if e == 0 else rest + own, axis=0))
            entering = dot(sorted_cot, jnp.concatenate(states, axis=1), NN)
            for e in range(2):
                h = 2 * j + e
                cum_t = jnp.broadcast_to(cum_g[:, h : h + 1], (BLOCK, BLOCK))
                decay = jnp.exp(jnp.minimum(cum_t - cum_rows[h : h + 1, :], 0.0))
                a = decay * inner[:, e * BLOCK : (e + 1) * BLOCK]
                step_s = step_rows[h : h + 1, :]
                ds_ref[...] += a * step_s
                b = scores * a
                cols.append(jnp.sum(b, axis=0, keepdims=True))
                w = entering[:, e * BLOCK : (e + 1) * BLOCK] * jnp.exp(cum_t)
                dq_ref[...] += w
                total = jnp.sum(b * step_s + w * query_twice, axis=1, keepdims=True)
                rows = jnp.where(s_index == h, total, rows)
        row_groups[g] = rows
        col_t[pl.ds(at, GROUP), :] = jnp.concatenate(cols, axis=0)

    dcum = row_groups[0]
    for g in range(1, HEADS // GROUP):
        dcum = dcum + pltpu.roll(row_groups[g], GROUP * g, 1)
    dstep = col_t[...].T[:, :HEADS]
    dcum = dcum[:, :HEADS] - step * dstep
    dstep = dstep - rate * dot(upper, dcum, NN, EXACT)
    draw = dstep * jax.nn.sigmoid(raw)
    dscores = jnp.where(causal, ds_ref[...], 0.0)
    dquery = dot(dscores, key, NN, EXACT) + dq_ref[:, :STATE] + dq_ref[:, STATE:]
    dkey = dot(dscores.T, query, NN, EXACT)
    keys = jnp.concatenate([dkey, dquery], axis=1)
    steps = jnp.concatenate([draw, jnp.zeros_like(draw)], axis=1)
    grad_ref[: 2 * STATE, :] = keys.T.astype(BF16)
    grad_ref[2 * STATE :, :] = steps.T[:HEADS, :].astype(BF16)
    keys16 = keys.astype(BF16)
    steps16 = draw.astype(BF16)

    @pl.loop(0, D // 512)
    def _(i):
        lanes = pl.ds(pl.multiple_of(i * 512, 512), 512)
        product = dot(keys16, w_ref[: 2 * STATE, lanes], NN)
        product += dot(steps16, w_ref[2 * STATE :, lanes], NN)
        out_ref[:, lanes] = product.astype(BF16)


def block(block_input, values, cot, state, bias, decay, weights):
    vmem = pl.BlockSpec(memory_space=pltpu.VMEM)
    return pl.pallas_call(
        block_kernel,
        out_shape=(
            jax.ShapeDtypeStruct((BLOCK, D), BF16),
            jax.ShapeDtypeStruct((COLS, BLOCK), BF16),
        ),
        in_specs=[vmem] * 7,
        out_specs=(vmem, vmem),
        scratch_shapes=[
            pltpu.VMEM((HEADS // GROUP, BLOCK, BLOCK), F32),
            pltpu.VMEM((HEADS // GROUP, BLOCK, BLOCK), F32),
            pltpu.VMEM((BLOCK, BLOCK), F32),
            pltpu.VMEM((BLOCK, BLOCK), F32),
            pltpu.VMEM((BLOCK, BLOCK), F32),
            pltpu.VMEM((BLOCK, BLOCK), F32),
        ],
        name="block_backward",
    )(block_input, values, cot, state, bias, decay, weights)


def reduce_kernel(
    grad_ref, cols_ref, params_ref, global_ref, momentum_ref,
    new_params_ref, new_momentum_ref,
    grads, partial, from_z, to_y, from_y, share, shares, sem_send, sem_recv, sem_self,
):
    x, yl, yh, z, c = place()
    y = yh * NYL + yl
    me_q = x * NC + c

    def at_y(i):
        return lax.rem(i, NYL), lax.div(i, NYL)

    along_z = [device(x, yl, yh, shift(z, dz, NZ), c) for dz in range(1, NZ)]
    along_y = []
    for dy in range(1, NYL * NYH):
        tyl, tyh = at_y(shift(y, dy, NYL * NYH))
        along_y.append(device(x, tyl, tyh, z, c))
    greet(along_z + along_y + replica_group(x, yl, yh, z, c))

    def lanes(q):
        return pl.ds(pl.multiple_of(q * BLOCK, BLOCK), BLOCK)

    mine = grads.at[:, lanes(me_q)]
    for dx in (2, 1, 3, 0):
        for dc in range(NC):
            if (dx, dc) == (0, 0):
                pltpu.make_async_copy(grad_ref, mine, sem_recv.at[0]).start()
            else:
                remote(
                    grad_ref, mine, sem_send.at[0], sem_recv.at[0],
                    device(shift(x, dx, NX), yl, yh, z, shift(c, dc, NC)),
                ).start()
    held = params_ref[0]
    for r in range(1, NX * NYL):
        held = held + params_ref[r]
    wait_bytes(grads, sem_recv.at[0])

    products = dot(grads[...], cols_ref[...], NN)
    for b in range(NZ):
        partial[b] = products[16 * b : 16 * b + 16, :].astype(BF16)
    for dz in (6, 5, 7, 4, 8, 3, 9, 2, 10, 1, 11):
        tz = shift(z, dz, NZ)
        remote(
            partial.at[tz], from_z.at[z], sem_send.at[1], sem_recv.at[1],
            device(x, yl, yh, tz, c),
        ).start()
    pltpu.make_async_copy(partial.at[z], from_z.at[z], sem_recv.at[1]).start()
    wait_bytes(from_z, sem_recv.at[1])
    total = from_z[0].astype(F32)
    for b in range(1, NZ):
        total = total + from_z[b].astype(F32)
    for i in range(NYL * NYH):
        to_y[i] = total[2 * i : 2 * i + 2, :]
    for dy in (4, 3, 5, 2, 6, 1, 7):
        ty = shift(y, dy, NYL * NYH)
        tyl, tyh = at_y(ty)
        remote(
            to_y.at[ty], from_y.at[y], sem_send.at[2], sem_recv.at[2],
            device(x, tyl, tyh, z, c),
        ).start()
    pltpu.make_async_copy(to_y.at[y], from_y.at[y], sem_recv.at[2]).start()
    wait_bytes(from_y, sem_recv.at[2])
    summed = from_y[0]
    for i in range(1, NYL * NYH):
        summed = summed + from_y[i]
    share[...] = (inner_rate * summed - held) * (1.0 / (NX * NYL))
    own = yl == c
    for dx in (2, 1, 3, 0):
        for dy in range(NYL):
            tx, tyl = shift(x, dx, NX), shift(yl, dy, NYL)
            dst = shares.at[me_q]
            if (dx, dy) == (0, 0):
                pl.when(own)(pltpu.make_async_copy(share, dst, sem_recv.at[3]).start)
                copy = remote(
                    share, dst, sem_self, sem_recv.at[3], device(tx, tyl, yh, z, 1 - c)
                )
                pl.when(jnp.logical_not(own))(copy.start)
            else:
                remote(
                    share, dst, sem_send.at[3], sem_recv.at[3], device(tx, tyl, yh, z, yl)
                ).start()
    wait_bytes(shares, sem_recv.at[3])
    for q in range(NX * NC):
        cols = slice(q * SLICE, (q + 1) * SLICE)
        outer = global_ref[:, cols]
        mean_pseudo = outer + shares[q]
        momentum = momentum_decay * momentum_ref[:, cols] + mean_pseudo
        new_momentum_ref[:, cols] = momentum
        new_params_ref[:, cols] = outer - outer_rate * (mean_pseudo + momentum_decay * momentum)
    wait_bytes(grads.at[:, : 7 * BLOCK], sem_send.at[0])
    wait_bytes(from_z.at[: NZ - 1], sem_send.at[1])
    wait_bytes(from_y.at[:7], sem_send.at[2])
    wait_bytes(shares.at[:7], sem_send.at[3])

    @pl.when(jnp.logical_not(own))
    def _():
        wait_bytes(share, sem_self)


def reduce(grad, cols, params, global_params, momentum):
    vmem = pl.BlockSpec(memory_space=pltpu.VMEM)
    return pl.pallas_call(
        reduce_kernel,
        out_shape=(
            jax.ShapeDtypeStruct((2, D), F32),
            jax.ShapeDtypeStruct((2, D), F32),
        ),
        in_specs=[vmem] * 5,
        out_specs=(vmem, vmem),
        scratch_shapes=[
            pltpu.VMEM((COLS, NX * NC * BLOCK), BF16),
            pltpu.VMEM((NZ, COLS // NZ, SLICE), BF16),
            pltpu.VMEM((NZ, COLS // NZ, SLICE), BF16),
            pltpu.VMEM((NYL * NYH, 2, SLICE), F32),
            pltpu.VMEM((NYL * NYH, 2, SLICE), F32),
            pltpu.VMEM((2, SLICE), F32),
            pltpu.VMEM((NX * NC, 2, SLICE), F32),
            pltpu.SemaphoreType.DMA((4,)),
            pltpu.SemaphoreType.DMA((4,)),
            pltpu.SemaphoreType.DMA,
        ],
        compiler_params=pltpu.CompilerParams(collective_id=1, has_side_effects=True),
        name="reduce_and_step",
    )(grad, cols, params, global_params, momentum)


def on_device(
    block_input, ssd_input, out_grad, start_state, step_bias, decay_log,
    local_params, global_params, momentum,
):
    weights, cols, params = gather(local_params, block_input)
    block_grad, grad = block(
        block_input,
        ssd_input,
        out_grad,
        start_state.reshape(HEADS, STATE // 2, 2 * STATE),
        step_bias.reshape(1, HEADS),
        decay_log.reshape(1, HEADS),
        weights.reshape(COLS, D),
    )
    new_params, new_momentum = reduce(
        grad, cols.reshape(NX * NC * BLOCK, SLICE), params, global_params, momentum
    )
    return block_grad, new_params, new_momentum


def solution(mesh):
    placed = (
        P(("rep", "fsdp"), None),
        P(("rep", "fsdp"), None),
        P(("rep", "fsdp"), None),
        P(("rep", "fsdp"), None, None),
        P(),
        P(),
        P("rep", "fsdp", None),
        P("fsdp", None),
        P("fsdp", None),
    )
    return jax.shard_map(
        on_device,
        mesh=mesh,
        in_specs=placed,
        out_specs=(P(("rep", "fsdp"), None), P("fsdp", None), P("fsdp", None)),
        check_vma=False,
    )
```

```python
import jax
import jax.numpy as jnp
from jax import lax
from jax.experimental import pallas as pl
from jax.experimental.pallas import tpu as pltpu
from jax.sharding import PartitionSpec as P

HEADS = 64
STATE = 64
BLOCK = 128
D = 4096
COLS = 192
NX, NYL, NYH, NZ, NC = 4, 2, 4, 12, 2
SLICE = D // (NX * NC)
HALF = D // NC
CHUNKS = 4
CHUNK = HALF // CHUNKS
RIGHT, LEFT = 6, 5

inner_rate = 0.002
outer_rate = 0.7
momentum_decay = 0.9

MESH = pl.DeviceIdType.MESH
F32 = jnp.float32
BF16 = jnp.bfloat16
EXACT = lax.Precision.HIGHEST


def place():
    rep = lax.axis_index("rep")
    fsdp = lax.axis_index("fsdp")
    x = lax.rem(rep, NX)
    yl = lax.div(rep, NX)
    z = lax.div(fsdp, NYH * NC)
    yh = lax.rem(lax.div(fsdp, NC), NYH)
    c = lax.rem(fsdp, NC)
    return x, yl, yh, z, c


def device(x, yl, yh, z, c):
    return (yl * NX + x, z * (NYH * NC) + yh * NC + c)


def shift(i, by, n):
    return lax.rem(i + by, n)


def replica_group(x, yl, yh, z, c):
    return [
        device(shift(x, dx, NX), shift(yl, dy, NYL), yh, z, shift(c, dc, NC))
        for dx in range(NX)
        for dy in range(NYL)
        for dc in range(NC)
        if (dx, dy, dc) != (0, 0, 0)
    ]


def remote(src, dst, send_sem, recv_sem, target):
    return pltpu.make_async_remote_copy(
        src_ref=src,
        dst_ref=dst,
        send_sem=send_sem,
        recv_sem=recv_sem,
        device_id=target,
        device_id_type=MESH,
    )


def wait_bytes(ref, sem):
    pltpu.make_async_copy(ref, ref, sem).wait()


def dot(a, b, dims, precision=None):
    return lax.dot_general(
        a, b, ((dims[0], dims[1]), ((), ())), precision=precision, preferred_element_type=F32
    )


NN = ((1,), (0,))
NT = ((1,), (1,))
TN = ((0,), (0,))
GROUP = 8

PAIRS = HEADS // 2
EARLY = PAIRS - CHUNKS * (RIGHT + 1)


def step_kernel(
    input_hbm, values_hbm, cot_hbm, state_hbm, bias_hbm, decay_hbm, rows_hbm,
    out_hbm, shares,
    bias_ref, decay_ref, out_ref,
    input_ref, values_ref, cot_ref, state_ref, state32, rows32, rows16, shards, block32,
    w_ref, cols_ref, params_ref, inner_ref, enter_ref,
    cum_groups, row_groups, both_t, col_t, ds_ref, dq_ref,
    mine, grads, partial, from_z, to_y, from_y, share,
    sem_load, sem_send, sem_recv, sem_x, ring_right, ring_left, sem_self,
):
    x, yl, yh, z, c = place()
    y = yh * NYL + yl
    me_a = yh * NC + c
    me_q = x * NC + c
    me_r = yl * NX + x
    own = yl == c

    def at_y(i):
        return lax.rem(i, NYL), lax.div(i, NYL)

    def half(core):
        return pl.ds(pl.multiple_of(core * HALF, HALF), HALF)

    def part(q):
        return pl.ds(pl.multiple_of(q * SLICE, SLICE), SLICE)

    def tokens(q):
        return pl.ds(pl.multiple_of(q * BLOCK, BLOCK), BLOCK)

    def rows_of(b):
        return pl.ds(pl.multiple_of(b * 16, 16), 16)

    loads = [
        pltpu.make_async_copy(src, dst, sem_load.at[i])
        for i, (src, dst) in enumerate(
            [
                (rows_hbm.at[0], rows32),
                (state_hbm.at[0], state_ref),
                (cot_hbm, cot_ref),
                (values_hbm, values_ref),
                (input_hbm, input_ref),
                (bias_hbm, bias_ref),
                (decay_hbm, decay_ref),
            ]
        )
    ]
    for load in loads:
        load.start()

    right = device(x, yl, yh, shift(z, 1, NZ), c)
    left = device(x, yl, yh, shift(z, NZ - 1, NZ), c)
    partner = device(x, yl, yh, z, 1 - c)
    along_z = [device(x, yl, yh, shift(z, dz, NZ), c) for dz in range(1, NZ)]
    along_y = []
    for dy in range(1, NYL * NYH):
        tyl, tyh = at_y(shift(y, dy, NYL * NYH))
        along_y.append(device(x, tyl, tyh, z, c))
    across = [device(x, yl, shift(yh, dy, NYH), z, 1 - c) for dy in range(1, NYH)]
    greeted = along_z + along_y + across + replica_group(x, yl, yh, z, c)
    barrier = pltpu.get_barrier_semaphore()
    for target in greeted:
        pl.semaphore_signal(barrier, inc=1, device_id=target, device_id_type=MESH)
    loads[0].wait()
    rows16[...] = rows32[...].astype(BF16)
    pl.semaphore_wait(barrier, len(greeted))

    for dy in (2, 1, 3, 0):
        for dc in range(NC):
            core = shift(c, dc, NC)
            src = rows16.at[:, half(core)]
            dst = shards.at[me_a]
            if (dy, dc) == (0, 0):
                pltpu.make_async_copy(src, dst, sem_recv.at[0]).start()
            else:
                remote(
                    src, dst, sem_send.at[0], sem_recv.at[0],
                    device(x, yl, shift(yh, dy, NYH), z, core),
                ).start()
    for dx in (2, 1, 3, 0):
        for dc in range(NC):
            tx, core = shift(x, dx, NX), shift(c, dc, NC)
            src = input_hbm.at[:, part(tx * NC + core)]
            dst = cols_ref.at[tokens(me_q)]
            if (dx, dc) == (0, 0):
                pltpu.make_async_copy(src, dst, sem_recv.at[1]).start()
            else:
                remote(
                    src, dst, sem_send.at[1], sem_recv.at[1], device(tx, yl, yh, z, core)
                ).start()
    for dx in (2, 1, 3, 0):
        for dc in range(NC):
            tx, core = shift(x, dx, NX), shift(c, dc, NC)
            src = rows32.at[:, part(tx * NC + core)]
            dst = params_ref.at[me_r]
            if (dx, dc) == (0, 0):
                pl.when(own)(pltpu.make_async_copy(src, dst, sem_recv.at[2]).start)
                copy = remote(
                    src, dst, sem_self.at[0], sem_recv.at[2], device(tx, 1 - yl, yh, z, core)
                )
                pl.when(jnp.logical_not(own))(copy.start)
            else:
                remote(
                    src, dst, sem_send.at[2], sem_recv.at[2], device(tx, c, yh, z, core)
                ).start()

    t_index = lax.broadcasted_iota(jnp.int32, (BLOCK, BLOCK), 0)
    s_index = lax.broadcasted_iota(jnp.int32, (BLOCK, BLOCK), 1)
    first = s_index < STATE
    column = lax.rem(s_index, STATE)
    origin = (s_index - column) + 2 * lax.rem(column, STATE // 2) + lax.div(column, STATE // 2)
    order = jnp.where(t_index == origin, 1.0, 0.0).astype(BF16)
    low = lax.broadcasted_iota(jnp.int32, (STATE // 2, BLOCK), 1) < STATE
    zero_state = jnp.zeros((STATE // 2, BLOCK), BF16)

    def products(p):
        lanes = tokens(p)
        cot = cot_ref[:, lanes]
        val = values_ref[:, lanes]
        zero = jnp.zeros_like(val)
        pair = jnp.concatenate(
            [jnp.where(first, val, zero), jnp.where(first, zero, val)], axis=0
        )
        inner_ref[p] = dot(cot, pair, NT)
        sorted_cot = dot(cot, order, NN).astype(BF16)
        states = []
        for e in range(2):
            st = state32[pl.ds(2 * p + e, STATE // 2, stride=HEADS), :].astype(BF16)
            kept = [jnp.where(low, st, zero_state), jnp.where(low, zero_state, st)]
            rest = [zero_state, zero_state]
            states.append(jnp.concatenate(kept + rest if e == 0 else rest + kept, axis=0))
        enter_ref[p] = dot(sorted_cot, jnp.concatenate(states, axis=1), NN)

    for load in loads[1:]:
        load.wait()
    for j in range(STATE // 2):
        state32[j * HEADS : (j + 1) * HEADS, :] = state_ref[:, j * BLOCK : (j + 1) * BLOCK].astype(F32)
    wait_bytes(shards, sem_recv.at[0])
    for i in range(NYH * NC):
        block32[2 * i : 2 * i + 2, :] = shards[i].astype(F32)
    w_ref[rows_of(z), half(c)] = block32[...].astype(BF16)

    def chunk(b, k):
        return w_ref.at[rows_of(b), pl.ds(pl.multiple_of(c * HALF + k * CHUNK, CHUNK), CHUNK)]

    def pass_on(b):
        block = w_ref.at[rows_of(b), half(c)]
        remote(block, block, sem_send.at[4], sem_recv.at[3], partner).start()

    @pl.loop(0, RIGHT + 1)
    def _(s):
        br = lax.rem(z + NZ - s, NZ)
        bl = lax.rem(z + s, NZ)
        before = jnp.maximum(s - 1, 0)
        for k in range(CHUNKS):
            to_right = chunk(br, k)
            to_left = chunk(bl, k)

            @pl.when(s > 0)
            def _():
                remote(
                    to_right, to_right, sem_send.at[3], ring_right.at[before, k], right
                ).wait_recv()

            @pl.when(s < RIGHT)
            def _():
                remote(
                    to_right, to_right, sem_send.at[3], ring_right.at[s, k], right
                ).start()

            @pl.when(jnp.logical_and(s > 0, s <= LEFT))
            def _():
                remote(
                    to_left, to_left, sem_send.at[3], ring_left.at[before, k], left
                ).wait_recv()

            @pl.when(s < LEFT)
            def _():
                remote(
                    to_left, to_left, sem_send.at[3], ring_left.at[s, k], left
                ).start()

            products(s * CHUNKS + k)

        pass_on(br)

        @pl.when(jnp.logical_and(s > 0, s <= LEFT))
        def _():
            pass_on(bl)

    for p in range(PAIRS - EARLY, PAIRS):
        products(p)
    wait_bytes(w_ref.at[:, half(1 - c)], sem_recv.at[3])

    proj = dot(input_ref[...], w_ref[...], NT)
    key = proj[:, :STATE]
    query = proj[:, STATE : 2 * STATE]
    raw = proj[:, 2 * STATE :] + bias_ref[...]
    rate = jnp.exp(decay_ref[...])
    step = jnp.maximum(raw, 0.0) + jnp.log1p(jnp.exp(-jnp.abs(raw)))
    causal = t_index >= s_index
    lower = jnp.where(causal, 1.0, 0.0)
    upper = jnp.where(t_index <= s_index, 1.0, 0.0)
    cum = dot(lower, -step * rate, NN, EXACT)
    wide = jnp.concatenate([cum, step], axis=1)
    both_t[...] = wide.T
    for g in range(HEADS // GROUP):
        cum_groups[g] = pltpu.roll(wide, (BLOCK - GROUP * g) % BLOCK, 1) if g else wide
    scores = jnp.where(causal, dot(query, key, NT, EXACT), 0.0)
    query_twice = jnp.concatenate([query, query], axis=1)
    ds_ref[...] = jnp.zeros_like(ds_ref)
    dq_ref[...] = jnp.zeros_like(dq_ref)

    @pl.loop(0, HEADS // GROUP)
    def _(g):
        cum_g = cum_groups[g]
        at = pl.multiple_of(g * GROUP, GROUP)
        cum_rows = both_t[pl.ds(at, GROUP), :]
        step_rows = both_t[pl.ds(HEADS + at, GROUP), :]
        rows = jnp.zeros((BLOCK, BLOCK), F32)
        cols = []
        for h in range(GROUP):
            p = g * (GROUP // 2) + h // 2
            lanes = slice((h % 2) * BLOCK, (h % 2 + 1) * BLOCK)
            cum_t = jnp.broadcast_to(cum_g[:, h : h + 1], (BLOCK, BLOCK))
            decay = jnp.exp(jnp.minimum(cum_t - cum_rows[h : h + 1, :], 0.0))
            a = decay * inner_ref[p, :, lanes]
            step_s = step_rows[h : h + 1, :]
            ds_ref[...] += a * step_s
            b = scores * a
            cols.append(jnp.sum(b, axis=0, keepdims=True))
            w = enter_ref[p, :, lanes] * jnp.exp(cum_t)
            dq_ref[...] += w
            total = jnp.sum(b * step_s + w * query_twice, axis=1, keepdims=True)
            rows = jnp.where(s_index == h, total, rows)
        row_groups[g] = rows
        col_t[pl.ds(at, GROUP), :] = jnp.concatenate(cols, axis=0)

    dcum = row_groups[0]
    for g in range(1, HEADS // GROUP):
        dcum = dcum + pltpu.roll(row_groups[g], GROUP * g, 1)
    dstep = col_t[...].T[:, :HEADS]
    dcum = dcum[:, :HEADS] - step * dstep
    dstep = dstep - rate * dot(upper, dcum, NN, EXACT)
    draw = dstep * jax.nn.sigmoid(raw)
    dscores = jnp.where(causal, ds_ref[...], 0.0)
    dquery = dot(dscores, key, NN, EXACT) + dq_ref[:, :STATE] + dq_ref[:, STATE:]
    dkey = dot(dscores.T, query, NN, EXACT)
    keys = jnp.concatenate([dkey, dquery], axis=1)
    steps = jnp.concatenate([draw, jnp.zeros_like(draw)], axis=1)
    mine[: 2 * STATE, :] = keys.T.astype(BF16)
    mine[2 * STATE :, :] = steps.T[:HEADS, :].astype(BF16)

    here = grads.at[:, tokens(me_q)]
    for dx in (2, 1, 3):
        remote(
            mine, here, sem_send.at[5], sem_x.at[dx], device(shift(x, dx, NX), yl, yh, z, c)
        ).start()
    remote(mine, here, sem_send.at[9], sem_recv.at[4], partner).start()
    pltpu.make_async_copy(mine, here, sem_x.at[0]).start()

    keys16 = keys.astype(BF16)
    steps16 = draw.astype(BF16)

    @pl.loop(0, D // 512)
    def _(i):
        lanes = pl.ds(pl.multiple_of(i * 512, 512), 512)
        product = dot(keys16, w_ref[: 2 * STATE, lanes], NN)
        product += dot(steps16, w_ref[2 * STATE :, lanes], NN)
        out_ref[:, lanes] = product.astype(BF16)
        pltpu.make_async_copy(out_ref.at[:, lanes], out_hbm.at[:, lanes], sem_load.at[7]).start()

    for dx in (1, 3, 2):
        there = grads.at[:, tokens(shift(x, NX - dx, NX) * NC + c)]
        copy = remote(there, there, sem_send.at[9], sem_x.at[dx], partner)
        copy.wait_recv()
        remote(there, there, sem_send.at[9], sem_recv.at[4], partner).start()
    wait_bytes(here, sem_x.at[0])
    wait_bytes(cols_ref, sem_recv.at[1])
    wait_bytes(params_ref, sem_recv.at[2])
    held = params_ref[0]
    for r in range(1, NX * NYL):
        held = held + params_ref[r]
    wait_bytes(grads.at[:, : NX * BLOCK], sem_recv.at[4])

    gradient = dot(grads[...], cols_ref[...], NN)
    for b in range(NZ):
        partial[b] = gradient[16 * b : 16 * b + 16, :].astype(BF16)
    for dz in (6, 5, 7, 4, 8, 3, 9, 2, 10, 1, 11):
        tz = shift(z, dz, NZ)
        remote(
            partial.at[tz], from_z.at[z], sem_send.at[6], sem_recv.at[5],
            device(x, yl, yh, tz, c),
        ).start()
    pltpu.make_async_copy(partial.at[z], from_z.at[z], sem_recv.at[5]).start()
    wait_bytes(from_z, sem_recv.at[5])
    total = from_z[0].astype(F32)
    for b in range(1, NZ):
        total = total + from_z[b].astype(F32)
    for i in range(NYL * NYH):
        to_y[i] = total[2 * i : 2 * i + 2, :]
    for dy in (4, 3, 5, 2, 6, 1, 7):
        ty = shift(y, dy, NYL * NYH)
        tyl, tyh = at_y(ty)
        remote(
            to_y.at[ty], from_y.at[y], sem_send.at[7], sem_recv.at[6],
            device(x, tyl, tyh, z, c),
        ).start()
    pltpu.make_async_copy(to_y.at[y], from_y.at[y], sem_recv.at[6]).start()
    wait_bytes(from_y, sem_recv.at[6])
    summed = from_y[0]
    for i in range(1, NYL * NYH):
        summed = summed + from_y[i]
    share[...] = (inner_rate * summed - held) * (1.0 / (NX * NYL))
    for dx in (2, 1, 3, 0):
        for dy in range(NYL):
            tx, tyl = shift(x, dx, NX), shift(yl, dy, NYL)
            dst = shares.at[me_q]
            if (dx, dy) == (0, 0):
                pl.when(own)(pltpu.make_async_copy(share, dst, sem_recv.at[7]).start)
                copy = remote(
                    share, dst, sem_self.at[1], sem_recv.at[7], device(tx, tyl, yh, z, 1 - c)
                )
                pl.when(jnp.logical_not(own))(copy.start)
            else:
                remote(
                    share, dst, sem_send.at[8], sem_recv.at[7], device(tx, tyl, yh, z, yl)
                ).start()
    wait_bytes(shards.at[0:7], sem_send.at[0])
    wait_bytes(cols_ref.at[0 : 7 * BLOCK], sem_send.at[1])
    wait_bytes(params_ref.at[0:7], sem_send.at[2])
    wait_bytes(w_ref.at[0 : 16 * (RIGHT + LEFT), half(c)], sem_send.at[3])
    wait_bytes(w_ref.at[:, half(c)], sem_send.at[4])
    wait_bytes(grads.at[:, : 3 * BLOCK], sem_send.at[5])
    wait_bytes(grads.at[:, : NX * BLOCK], sem_send.at[9])
    wait_bytes(from_z.at[: NZ - 1], sem_send.at[6])
    wait_bytes(from_y.at[:7], sem_send.at[7])

    @pl.when(jnp.logical_not(own))
    def _():
        wait_bytes(params_ref.at[0], sem_self.at[0])
        wait_bytes(share, sem_self.at[1])

    wait_bytes(out_ref, sem_load.at[7])
    wait_bytes(shares, sem_recv.at[7])
    wait_bytes(shares.at[:7], sem_send.at[8])


def step(block_input, values, cot, state, bias, decay, rows):
    vmem = pl.BlockSpec(memory_space=pltpu.VMEM)
    hbm = pl.BlockSpec(memory_space=pl.ANY)
    square = pltpu.VMEM((BLOCK, BLOCK), F32)
    groups = pltpu.VMEM((HEADS // GROUP, BLOCK, BLOCK), F32)
    return pl.pallas_call(
        step_kernel,
        out_shape=(
            jax.ShapeDtypeStruct((BLOCK, D), BF16),
            jax.ShapeDtypeStruct((NX * NC, 2, SLICE), F32),
        ),
        in_specs=[hbm] * 7,
        out_specs=(hbm, vmem),
        scratch_shapes=[
            pltpu.VMEM((1, HEADS), F32),
            pltpu.VMEM((1, HEADS), F32),
            pltpu.VMEM((BLOCK, D), BF16),
            pltpu.VMEM((BLOCK, D), BF16),
            pltpu.VMEM((BLOCK, D), BF16),
            pltpu.VMEM((BLOCK, D), BF16),
            pltpu.VMEM((HEADS, D), BF16),
            pltpu.VMEM((HEADS * STATE // 2, BLOCK), F32),
            pltpu.VMEM((2, D), F32),
            pltpu.VMEM((2, D), BF16),
            pltpu.VMEM((NYH * NC, 2, HALF), BF16),
            pltpu.VMEM((COLS // NZ, HALF), F32),
            pltpu.VMEM((COLS, D), BF16),
            pltpu.VMEM((NX * NC * BLOCK, SLICE), BF16),
            pltpu.VMEM((NX * NYL, 2, SLICE), F32),
            pltpu.VMEM((PAIRS, BLOCK, 2 * BLOCK), F32),
            pltpu.VMEM((PAIRS, BLOCK, 2 * BLOCK), F32),
            groups,
            groups,
            square,
            pltpu.VMEM((HEADS, BLOCK), F32),
            square,
            square,
            pltpu.VMEM((COLS, BLOCK), BF16),
            pltpu.VMEM((COLS, NX * NC * BLOCK), BF16),
            pltpu.VMEM((NZ, COLS // NZ, SLICE), BF16),
            pltpu.VMEM((NZ, COLS // NZ, SLICE), BF16),
            pltpu.VMEM((NYL * NYH, 2, SLICE), F32),
            pltpu.VMEM((NYL * NYH, 2, SLICE), F32),
            pltpu.VMEM((2, SLICE), F32),
            pltpu.SemaphoreType.DMA((8,)),
            pltpu.SemaphoreType.DMA((10,)),
            pltpu.SemaphoreType.DMA((8,)),
            pltpu.SemaphoreType.DMA((NX,)),
            pltpu.SemaphoreType.DMA((RIGHT, CHUNKS)),
            pltpu.SemaphoreType.DMA((LEFT, CHUNKS)),
            pltpu.SemaphoreType.DMA((2,)),
        ],
        compiler_params=pltpu.CompilerParams(
            collective_id=0, has_side_effects=True, vmem_limit_bytes=62 << 20
        ),
        name="block_step",
    )(block_input, values, cot, state, bias, decay, rows)


def outer_kernel(
    grad_hbm, shares_ref, global_ref, momentum_ref,
    out_hbm, new_params_ref, new_momentum_ref, held, sem_in, sem_out,
):
    width = D // 4
    cuts = [slice(i * width, (i + 1) * width) for i in range(4)]
    takes = [
        pltpu.make_async_copy(grad_hbm.at[:, cut], held.at[:, cut], sem_in.at[i])
        for i, cut in enumerate(cuts)
    ]
    gives = [
        pltpu.make_async_copy(held.at[:, cut], out_hbm.at[:, cut], sem_out.at[i])
        for i, cut in enumerate(cuts)
    ]
    for take in takes:
        take.start()
    for take, give in zip(takes, gives):
        take.wait()
        give.start()
    for q in range(NX * NC):
        cols = slice(q * SLICE, (q + 1) * SLICE)
        outer = global_ref[:, cols]
        mean_pseudo = outer + shares_ref[q]
        momentum = momentum_decay * momentum_ref[:, cols] + mean_pseudo
        new_momentum_ref[:, cols] = momentum
        new_params_ref[:, cols] = outer - outer_rate * (mean_pseudo + momentum_decay * momentum)
    for give in gives:
        give.wait()


def outer(grad, shares, global_params, momentum):
    vmem = pl.BlockSpec(memory_space=pltpu.VMEM)
    hbm = pl.BlockSpec(memory_space=pl.ANY)
    return pl.pallas_call(
        outer_kernel,
        out_shape=(
            jax.ShapeDtypeStruct((BLOCK, D), BF16),
            jax.ShapeDtypeStruct((2, D), F32),
            jax.ShapeDtypeStruct((2, D), F32),
        ),
        in_specs=[hbm, vmem, vmem, vmem],
        out_specs=(hbm, vmem, vmem),
        scratch_shapes=[
            pltpu.VMEM((BLOCK, D), BF16),
            pltpu.SemaphoreType.DMA((4,)),
            pltpu.SemaphoreType.DMA((4,)),
        ],
        compiler_params=pltpu.CompilerParams(vmem_limit_bytes=62 << 20),
        name="outer_step",
    )(grad, shares, global_params, momentum)


def on_device(
    block_input, ssd_input, out_grad, start_state, step_bias, decay_log,
    local_params, global_params, momentum,
):
    grad, shares = step(
        block_input,
        ssd_input,
        out_grad,
        start_state,
        step_bias.reshape(1, HEADS),
        decay_log.reshape(1, HEADS),
        local_params,
    )
    return outer(grad, shares, global_params, momentum)


def solution(mesh):
    placed = (
        P(("rep", "fsdp"), None),
        P(("rep", "fsdp"), None),
        P(("rep", "fsdp"), None),
        P(("rep", "fsdp"), None, None),
        P(),
        P(),
        P("rep", "fsdp", None),
        P("fsdp", None),
        P("fsdp", None),
    )
    return jax.shard_map(
        on_device,
        mesh=mesh,
        in_specs=placed,
        out_specs=(P(("rep", "fsdp"), None), P("fsdp", None), P("fsdp", None)),
        check_vma=False,
    )
```

```python
import jax
import jax.numpy as jnp
from jax import lax
from jax.experimental import pallas as pl
from jax.experimental.pallas import tpu as pltpu
from jax.sharding import PartitionSpec as P

HEADS = 64
STATE = 64
BLOCK = 128
D = 4096
COLS = 192
NX, NYL, NYH, NZ, NC = 4, 2, 4, 12, 2
SLICE = D // (NX * NC)
HALF = D // NC
CHUNKS = 4
CHUNK = HALF // CHUNKS
STAGES = 3

inner_rate = 0.002
outer_rate = 0.7
momentum_decay = 0.9

MESH = pl.DeviceIdType.MESH
F32 = jnp.float32
BF16 = jnp.bfloat16
EXACT = lax.Precision.HIGHEST


def place():
    rep = lax.axis_index("rep")
    fsdp = lax.axis_index("fsdp")
    x = lax.rem(rep, NX)
    yl = lax.div(rep, NX)
    z = lax.div(fsdp, NYH * NC)
    yh = lax.rem(lax.div(fsdp, NC), NYH)
    c = lax.rem(fsdp, NC)
    return x, yl, yh, z, c


def device(x, yl, yh, z, c):
    return (yl * NX + x, z * (NYH * NC) + yh * NC + c)


def shift(i, by, n):
    return lax.rem(i + by, n)


def replica_group(x, yl, yh, z, c):
    return [
        device(shift(x, dx, NX), shift(yl, dy, NYL), yh, z, shift(c, dc, NC))
        for dx in range(NX)
        for dy in range(NYL)
        for dc in range(NC)
        if (dx, dy, dc) != (0, 0, 0)
    ]


def remote(src, dst, send_sem, recv_sem, target):
    return pltpu.make_async_remote_copy(
        src_ref=src,
        dst_ref=dst,
        send_sem=send_sem,
        recv_sem=recv_sem,
        device_id=target,
        device_id_type=MESH,
    )


def wait_bytes(ref, sem):
    pltpu.make_async_copy(ref, ref, sem).wait()


def dot(a, b, dims, precision=None):
    return lax.dot_general(
        a, b, ((dims[0], dims[1]), ((), ())), precision=precision, preferred_element_type=F32
    )


NN = ((1,), (0,))
NT = ((1,), (1,))
TN = ((0,), (0,))
GROUP = 8

PAIRS = HEADS // 2
EARLY = PAIRS - 2 * CHUNKS * STAGES


def step_kernel(
    input_hbm, values_hbm, cot_hbm, state_hbm, bias_hbm, decay_hbm, rows_hbm,
    out_hbm, shares,
    bias_ref, decay_ref, out_ref,
    input_ref, values_ref, cot_ref, state_ref, state32, rows32, rows16, shards, block32,
    w_ref, cols_ref, params_ref, inner_ref, enter_ref,
    cum_groups, row_groups, both_t, col_t, ds_ref, dq_ref,
    mine, grads, partial, from_z, to_y, from_y, share,
    sem_load, sem_send, sem_recv, sem_x, ring_right, ring_left, sem_self,
):
    x, yl, yh, z, c = place()
    y = yh * NYL + yl
    me_a = yh * NC + c
    me_q = x * NC + c
    me_r = yl * NX + x
    own = yl == c

    def at_y(i):
        return lax.rem(i, NYL), lax.div(i, NYL)

    def half(core):
        return pl.ds(pl.multiple_of(core * HALF, HALF), HALF)

    def part(q):
        return pl.ds(pl.multiple_of(q * SLICE, SLICE), SLICE)

    def tokens(q):
        return pl.ds(pl.multiple_of(q * BLOCK, BLOCK), BLOCK)

    def rows_of(b):
        return pl.ds(pl.multiple_of(b * 16, 16), 16)

    loads = [
        pltpu.make_async_copy(src, dst, sem_load.at[i])
        for i, (src, dst) in enumerate(
            [
                (rows_hbm.at[0], rows32),
                (state_hbm.at[0], state_ref),
                (cot_hbm, cot_ref),
                (values_hbm, values_ref),
                (input_hbm, input_ref),
                (bias_hbm, bias_ref),
                (decay_hbm, decay_ref),
            ]
        )
    ]
    for load in loads:
        load.start()

    right = device(x, yl, yh, shift(z, 1, NZ), c)
    left = device(x, yl, yh, shift(z, NZ - 1, NZ), c)
    right2 = device(x, yl, yh, shift(z, 2, NZ), c)
    left2 = device(x, yl, yh, shift(z, NZ - 2, NZ), c)
    partner = device(x, yl, yh, z, 1 - c)
    along_z = [device(x, yl, yh, shift(z, dz, NZ), c) for dz in range(1, NZ)]
    along_y = []
    for dy in range(1, NYL * NYH):
        tyl, tyh = at_y(shift(y, dy, NYL * NYH))
        along_y.append(device(x, tyl, tyh, z, c))
    across = [device(x, yl, shift(yh, dy, NYH), z, 1 - c) for dy in range(1, NYH)]
    greeted = along_z + along_y + across + replica_group(x, yl, yh, z, c)
    barrier = pltpu.get_barrier_semaphore()
    for target in greeted:
        pl.semaphore_signal(barrier, inc=1, device_id=target, device_id_type=MESH)
    loads[0].wait()
    rows16[...] = rows32[...].astype(BF16)
    pl.semaphore_wait(barrier, len(greeted))

    for dy in (2, 1, 3, 0):
        for dc in range(NC):
            core = shift(c, dc, NC)
            src = rows16.at[:, half(core)]
            dst = shards.at[me_a]
            if (dy, dc) == (0, 0):
                pltpu.make_async_copy(src, dst, sem_recv.at[0]).start()
            else:
                remote(
                    src, dst, sem_send.at[0], sem_recv.at[0],
                    device(x, yl, shift(yh, dy, NYH), z, core),
                ).start()
    for dx in (2, 1, 3, 0):
        for dc in range(NC):
            tx, core = shift(x, dx, NX), shift(c, dc, NC)
            src = input_hbm.at[:, part(tx * NC + core)]
            dst = cols_ref.at[tokens(me_q)]
            if (dx, dc) == (0, 0):
                pltpu.make_async_copy(src, dst, sem_recv.at[1]).start()
            else:
                remote(
                    src, dst, sem_send.at[1], sem_recv.at[1], device(tx, yl, yh, z, core)
                ).start()
    for dx in (2, 1, 3, 0):
        for dc in range(NC):
            tx, core = shift(x, dx, NX), shift(c, dc, NC)
            src = rows32.at[:, part(tx * NC + core)]
            dst = params_ref.at[me_r]
            if (dx, dc) == (0, 0):
                pl.when(own)(pltpu.make_async_copy(src, dst, sem_recv.at[2]).start)
                copy = remote(
                    src, dst, sem_self.at[0], sem_recv.at[2], device(tx, 1 - yl, yh, z, core)
                )
                pl.when(jnp.logical_not(own))(copy.start)
            else:
                remote(
                    src, dst, sem_send.at[2], sem_recv.at[2], device(tx, c, yh, z, core)
                ).start()

    t_index = lax.broadcasted_iota(jnp.int32, (BLOCK, BLOCK), 0)
    s_index = lax.broadcasted_iota(jnp.int32, (BLOCK, BLOCK), 1)
    first = s_index < STATE
    column = lax.rem(s_index, STATE)
    origin = (s_index - column) + 2 * lax.rem(column, STATE // 2) + lax.div(column, STATE // 2)
    order = jnp.where(t_index == origin, 1.0, 0.0).astype(BF16)
    low = lax.broadcasted_iota(jnp.int32, (STATE // 2, BLOCK), 1) < STATE
    zero_state = jnp.zeros((STATE // 2, BLOCK), BF16)

    def products(p):
        lanes = tokens(p)
        cot = cot_ref[:, lanes]
        val = values_ref[:, lanes]
        zero = jnp.zeros_like(val)
        pair = jnp.concatenate(
            [jnp.where(first, val, zero), jnp.where(first, zero, val)], axis=0
        )
        inner_ref[p] = dot(cot, pair, NT)
        sorted_cot = dot(cot, order, NN).astype(BF16)
        states = []
        for e in range(2):
            st = state32[pl.ds(2 * p + e, STATE // 2, stride=HEADS), :].astype(BF16)
            kept = [jnp.where(low, st, zero_state), jnp.where(low, zero_state, st)]
            rest = [zero_state, zero_state]
            states.append(jnp.concatenate(kept + rest if e == 0 else rest + kept, axis=0))
        enter_ref[p] = dot(sorted_cot, jnp.concatenate(states, axis=1), NN)

    for load in loads[1:]:
        load.wait()
    for j in range(STATE // 2):
        state32[j * HEADS : (j + 1) * HEADS, :] = state_ref[:, j * BLOCK : (j + 1) * BLOCK].astype(F32)
    for p in range(PAIRS - EARLY, PAIRS):
        products(p)
    wait_bytes(shards, sem_recv.at[0])
    for i in range(NYH * NC):
        block32[2 * i : 2 * i + 2, :] = shards[i].astype(F32)
    w_ref[rows_of(z), half(c)] = block32[...].astype(BF16)

    def chunk(b, k):
        return w_ref.at[rows_of(b), pl.ds(pl.multiple_of(c * HALF + k * CHUNK, CHUNK), CHUNK)]

    def pass_on(b):
        block = w_ref.at[rows_of(b), half(c)]
        remote(block, block, sem_send.at[4], sem_recv.at[3], partner).start()

    def hop(b, k, sem, target):
        piece = chunk(b, k)
        return remote(piece, piece, sem_send.at[3], sem, target)

    @pl.loop(0, STAGES)
    def _(s):
        br = lax.rem(z + NZ - 2 * s, NZ)
        bl = lax.rem(z + 2 * s, NZ)
        for k in range(CHUNKS):
            pl.when(s > 0)(hop(br, k, ring_right.at[2 * s, k], right).wait_recv)
            if k < CHUNKS // 2:
                hop(br, k, ring_right.at[2 * s + 2, k], right2).start()
            else:
                pl.when(s < STAGES - 1)(hop(br, k, ring_right.at[2 * s + 2, k], right2).start)
            hop(br, k, ring_right.at[2 * s + 1, k], right).start()
            pl.when(s > 0)(hop(bl, k, ring_left.at[2 * s, k], left).wait_recv)
            if k >= CHUNKS // 2:
                hop(bl, k, ring_left.at[2 * s + 2, k], left2).start()
            else:
                pl.when(s < STAGES - 1)(hop(bl, k, ring_left.at[2 * s + 2, k], left2).start)
            hop(bl, k, ring_left.at[2 * s + 1, k], left).start()
            products(s * 2 * CHUNKS + 2 * k)
            products(s * 2 * CHUNKS + 2 * k + 1)

        pass_on(br)

        @pl.when(s > 0)
        def _():
            pass_on(bl)
            fr = lax.rem(z + NZ + 1 - 2 * s, NZ)
            fl = lax.rem(z + 2 * s - 1, NZ)
            for k in range(CHUNKS):
                hop(fr, k, ring_right.at[2 * s - 1, k], right).wait_recv()
            pass_on(fr)
            for k in range(CHUNKS):
                hop(fl, k, ring_left.at[2 * s - 1, k], left).wait_recv()
            pass_on(fl)

    last = 2 * STAGES - 1
    fr, fl, far = shift(z, NZ - last, NZ), shift(z, last, NZ), shift(z, NZ // 2, NZ)
    for k in range(CHUNKS):
        hop(fr, k, ring_right.at[last, k], right).wait_recv()
    pass_on(fr)
    for k in range(CHUNKS):
        hop(fl, k, ring_left.at[last, k], left).wait_recv()
    pass_on(fl)
    for k in range(CHUNKS):
        ring = ring_right if k < CHUNKS // 2 else ring_left
        hop(far, k, ring.at[last + 1, k], right).wait_recv()
    pass_on(far)
    wait_bytes(w_ref.at[:, half(1 - c)], sem_recv.at[3])

    proj = dot(input_ref[...], w_ref[...], NT)
    key = proj[:, :STATE]
    query = proj[:, STATE : 2 * STATE]
    raw = proj[:, 2 * STATE :] + bias_ref[...]
    rate = jnp.exp(decay_ref[...])
    step = jnp.maximum(raw, 0.0) + jnp.log1p(jnp.exp(-jnp.abs(raw)))
    causal = t_index >= s_index
    lower = jnp.where(causal, 1.0, 0.0)
    upper = jnp.where(t_index <= s_index, 1.0, 0.0)
    cum = dot(lower, -step * rate, NN, EXACT)
    wide = jnp.concatenate([cum, step], axis=1)
    both_t[...] = wide.T
    for g in range(HEADS // GROUP):
        cum_groups[g] = pltpu.roll(wide, (BLOCK - GROUP * g) % BLOCK, 1) if g else wide
    scores = jnp.where(causal, dot(query, key, NT, EXACT), 0.0)
    query_twice = jnp.concatenate([query, query], axis=1)
    ds_ref[...] = jnp.zeros_like(ds_ref)
    dq_ref[...] = jnp.zeros_like(dq_ref)

    @pl.loop(0, HEADS // GROUP)
    def _(g):
        cum_g = cum_groups[g]
        at = pl.multiple_of(g * GROUP, GROUP)
        cum_rows = both_t[pl.ds(at, GROUP), :]
        step_rows = both_t[pl.ds(HEADS + at, GROUP), :]
        rows = jnp.zeros((BLOCK, BLOCK), F32)
        cols = []
        for h in range(GROUP):
            p = g * (GROUP // 2) + h // 2
            lanes = slice((h % 2) * BLOCK, (h % 2 + 1) * BLOCK)
            cum_t = jnp.broadcast_to(cum_g[:, h : h + 1], (BLOCK, BLOCK))
            decay = jnp.exp(jnp.minimum(cum_t - cum_rows[h : h + 1, :], 0.0))
            a = decay * inner_ref[p, :, lanes]
            step_s = step_rows[h : h + 1, :]
            ds_ref[...] += a * step_s
            b = scores * a
            cols.append(jnp.sum(b, axis=0, keepdims=True))
            w = enter_ref[p, :, lanes] * jnp.exp(cum_t)
            dq_ref[...] += w
            total = jnp.sum(b * step_s + w * query_twice, axis=1, keepdims=True)
            rows = jnp.where(s_index == h, total, rows)
        row_groups[g] = rows
        col_t[pl.ds(at, GROUP), :] = jnp.concatenate(cols, axis=0)

    dcum = row_groups[0]
    for g in range(1, HEADS // GROUP):
        dcum = dcum + pltpu.roll(row_groups[g], GROUP * g, 1)
    dstep = col_t[...].T[:, :HEADS]
    dcum = dcum[:, :HEADS] - step * dstep
    dstep = dstep - rate * dot(upper, dcum, NN, EXACT)
    draw = dstep * jax.nn.sigmoid(raw)
    dscores = jnp.where(causal, ds_ref[...], 0.0)
    dquery = dot(dscores, key, NN, EXACT) + dq_ref[:, :STATE] + dq_ref[:, STATE:]
    dkey = dot(dscores.T, query, NN, EXACT)
    keys = jnp.concatenate([dkey, dquery], axis=1)
    steps = jnp.concatenate([draw, jnp.zeros_like(draw)], axis=1)
    mine[: 2 * STATE, :] = keys.T.astype(BF16)
    mine[2 * STATE :, :] = steps.T[:HEADS, :].astype(BF16)

    here = grads.at[:, tokens(me_q)]
    for dx in (2, 1, 3):
        remote(
            mine, here, sem_send.at[5], sem_x.at[dx], device(shift(x, dx, NX), yl, yh, z, c)
        ).start()
    remote(mine, here, sem_send.at[9], sem_recv.at[4], partner).start()
    pltpu.make_async_copy(mine, here, sem_x.at[0]).start()

    keys16 = keys.astype(BF16)
    steps16 = draw.astype(BF16)

    @pl.loop(0, D // 512)
    def _(i):
        lanes = pl.ds(pl.multiple_of(i * 512, 512), 512)
        product = dot(keys16, w_ref[: 2 * STATE, lanes], NN)
        product += dot(steps16, w_ref[2 * STATE :, lanes], NN)
        out_ref[:, lanes] = product.astype(BF16)
        pltpu.make_async_copy(out_ref.at[:, lanes], out_hbm.at[:, lanes], sem_load.at[7]).start()

    for dx in (1, 3, 2):
        there = grads.at[:, tokens(shift(x, NX - dx, NX) * NC + c)]
        copy = remote(there, there, sem_send.at[9], sem_x.at[dx], partner)
        copy.wait_recv()
        remote(there, there, sem_send.at[9], sem_recv.at[4], partner).start()
    wait_bytes(here, sem_x.at[0])
    wait_bytes(cols_ref, sem_recv.at[1])
    wait_bytes(params_ref, sem_recv.at[2])
    held = params_ref[0]
    for r in range(1, NX * NYL):
        held = held + params_ref[r]
    wait_bytes(grads.at[:, : NX * BLOCK], sem_recv.at[4])

    gradient = dot(grads[...], cols_ref[...], NN)
    for b in range(NZ):
        partial[b] = gradient[16 * b : 16 * b + 16, :].astype(BF16)
    for dz in (6, 5, 7, 4, 8, 3, 9, 2, 10, 1, 11):
        tz = shift(z, dz, NZ)
        remote(
            partial.at[tz], from_z.at[z], sem_send.at[6], sem_recv.at[5],
            device(x, yl, yh, tz, c),
        ).start()
    pltpu.make_async_copy(partial.at[z], from_z.at[z], sem_recv.at[5]).start()
    wait_bytes(from_z, sem_recv.at[5])
    total = from_z[0].astype(F32)
    for b in range(1, NZ):
        total = total + from_z[b].astype(F32)
    for i in range(NYL * NYH):
        to_y[i] = total[2 * i : 2 * i + 2, :]
    for dy in (4, 3, 5, 2, 6, 1, 7):
        ty = shift(y, dy, NYL * NYH)
        tyl, tyh = at_y(ty)
        remote(
            to_y.at[ty], from_y.at[y], sem_send.at[7], sem_recv.at[6],
            device(x, tyl, tyh, z, c),
        ).start()
    pltpu.make_async_copy(to_y.at[y], from_y.at[y], sem_recv.at[6]).start()
    wait_bytes(from_y, sem_recv.at[6])
    summed = from_y[0]
    for i in range(1, NYL * NYH):
        summed = summed + from_y[i]
    share[...] = (inner_rate * summed - held) * (1.0 / (NX * NYL))
    for dx in (2, 1, 3, 0):
        for dy in range(NYL):
            tx, tyl = shift(x, dx, NX), shift(yl, dy, NYL)
            dst = shares.at[me_q]
            if (dx, dy) == (0, 0):
                pl.when(own)(pltpu.make_async_copy(share, dst, sem_recv.at[7]).start)
                copy = remote(
                    share, dst, sem_self.at[1], sem_recv.at[7], device(tx, tyl, yh, z, 1 - c)
                )
                pl.when(jnp.logical_not(own))(copy.start)
            else:
                remote(
                    share, dst, sem_send.at[8], sem_recv.at[7], device(tx, tyl, yh, z, yl)
                ).start()
    wait_bytes(shards.at[0:7], sem_send.at[0])
    wait_bytes(cols_ref.at[0 : 7 * BLOCK], sem_send.at[1])
    wait_bytes(params_ref.at[0:7], sem_send.at[2])
    wait_bytes(w_ref.at[0 : 16 * (NZ - 1), half(c)], sem_send.at[3])
    wait_bytes(w_ref.at[:, half(c)], sem_send.at[4])
    wait_bytes(grads.at[:, : 3 * BLOCK], sem_send.at[5])
    wait_bytes(grads.at[:, : NX * BLOCK], sem_send.at[9])
    wait_bytes(from_z.at[: NZ - 1], sem_send.at[6])
    wait_bytes(from_y.at[:7], sem_send.at[7])

    @pl.when(jnp.logical_not(own))
    def _():
        wait_bytes(params_ref.at[0], sem_self.at[0])
        wait_bytes(share, sem_self.at[1])

    wait_bytes(out_ref, sem_load.at[7])
    wait_bytes(shares, sem_recv.at[7])
    wait_bytes(shares.at[:7], sem_send.at[8])


def step(block_input, values, cot, state, bias, decay, rows):
    vmem = pl.BlockSpec(memory_space=pltpu.VMEM)
    hbm = pl.BlockSpec(memory_space=pl.ANY)
    square = pltpu.VMEM((BLOCK, BLOCK), F32)
    groups = pltpu.VMEM((HEADS // GROUP, BLOCK, BLOCK), F32)
    return pl.pallas_call(
        step_kernel,
        out_shape=(
            jax.ShapeDtypeStruct((BLOCK, D), BF16),
            jax.ShapeDtypeStruct((NX * NC, 2, SLICE), F32),
        ),
        in_specs=[hbm] * 7,
        out_specs=(hbm, vmem),
        scratch_shapes=[
            pltpu.VMEM((1, HEADS), F32),
            pltpu.VMEM((1, HEADS), F32),
            pltpu.VMEM((BLOCK, D), BF16),
            pltpu.VMEM((BLOCK, D), BF16),
            pltpu.VMEM((BLOCK, D), BF16),
            pltpu.VMEM((BLOCK, D), BF16),
            pltpu.VMEM((HEADS, D), BF16),
            pltpu.VMEM((HEADS * STATE // 2, BLOCK), F32),
            pltpu.VMEM((2, D), F32),
            pltpu.VMEM((2, D), BF16),
            pltpu.VMEM((NYH * NC, 2, HALF), BF16),
            pltpu.VMEM((COLS // NZ, HALF), F32),
            pltpu.VMEM((COLS, D), BF16),
            pltpu.VMEM((NX * NC * BLOCK, SLICE), BF16),
            pltpu.VMEM((NX * NYL, 2, SLICE), F32),
            pltpu.VMEM((PAIRS, BLOCK, 2 * BLOCK), F32),
            pltpu.VMEM((PAIRS, BLOCK, 2 * BLOCK), F32),
            groups,
            groups,
            square,
            pltpu.VMEM((HEADS, BLOCK), F32),
            square,
            square,
            pltpu.VMEM((COLS, BLOCK), BF16),
            pltpu.VMEM((COLS, NX * NC * BLOCK), BF16),
            pltpu.VMEM((NZ, COLS // NZ, SLICE), BF16),
            pltpu.VMEM((NZ, COLS // NZ, SLICE), BF16),
            pltpu.VMEM((NYL * NYH, 2, SLICE), F32),
            pltpu.VMEM((NYL * NYH, 2, SLICE), F32),
            pltpu.VMEM((2, SLICE), F32),
            pltpu.SemaphoreType.DMA((8,)),
            pltpu.SemaphoreType.DMA((10,)),
            pltpu.SemaphoreType.DMA((8,)),
            pltpu.SemaphoreType.DMA((NX,)),
            pltpu.SemaphoreType.DMA((2 * STAGES + 1, CHUNKS)),
            pltpu.SemaphoreType.DMA((2 * STAGES + 1, CHUNKS)),
            pltpu.SemaphoreType.DMA((2,)),
        ],
        compiler_params=pltpu.CompilerParams(
            collective_id=0, has_side_effects=True, vmem_limit_bytes=62 << 20
        ),
        name="block_step",
    )(block_input, values, cot, state, bias, decay, rows)


def outer_kernel(
    grad_hbm, shares_hbm, global_hbm, momentum_hbm,
    out_hbm, new_params_hbm, new_momentum_hbm,
    held, shares_ref, global_ref, momentum_ref, new_params_ref, new_momentum_ref, sem_in, sem_out,
):
    width = D // 4
    cuts = [slice(i * width, (i + 1) * width) for i in range(4)]
    small = [
        pltpu.make_async_copy(src, dst, sem_in.at[4 + i])
        for i, (src, dst) in enumerate(
            [(shares_hbm, shares_ref), (global_hbm, global_ref), (momentum_hbm, momentum_ref)]
        )
    ]
    takes = [
        pltpu.make_async_copy(grad_hbm.at[:, cut], held.at[:, cut], sem_in.at[i])
        for i, cut in enumerate(cuts)
    ]
    gives = [
        pltpu.make_async_copy(held.at[:, cut], out_hbm.at[:, cut], sem_out.at[i])
        for i, cut in enumerate(cuts)
    ]
    results = [
        pltpu.make_async_copy(new_params_ref, new_params_hbm, sem_out.at[4]),
        pltpu.make_async_copy(new_momentum_ref, new_momentum_hbm, sem_out.at[5]),
    ]
    for take in small + takes:
        take.start()
    for take in small:
        take.wait()
    for q in range(NX * NC):
        cols = slice(q * SLICE, (q + 1) * SLICE)
        outer = global_ref[:, cols]
        mean_pseudo = outer + shares_ref[q]
        momentum = momentum_decay * momentum_ref[:, cols] + mean_pseudo
        new_momentum_ref[:, cols] = momentum
        new_params_ref[:, cols] = outer - outer_rate * (mean_pseudo + momentum_decay * momentum)
    for result in results:
        result.start()
    for take, give in zip(takes, gives):
        take.wait()
        give.start()
    for give in gives + results:
        give.wait()


def outer(grad, shares, global_params, momentum):
    hbm = pl.BlockSpec(memory_space=pl.ANY)
    rows = pltpu.VMEM((2, D), F32)
    return pl.pallas_call(
        outer_kernel,
        out_shape=(
            jax.ShapeDtypeStruct((BLOCK, D), BF16),
            jax.ShapeDtypeStruct((2, D), F32),
            jax.ShapeDtypeStruct((2, D), F32),
        ),
        in_specs=[hbm] * 4,
        out_specs=(hbm, hbm, hbm),
        scratch_shapes=[
            pltpu.VMEM((BLOCK, D), BF16),
            pltpu.VMEM((NX * NC, 2, SLICE), F32),
            rows,
            rows,
            rows,
            rows,
            pltpu.SemaphoreType.DMA((7,)),
            pltpu.SemaphoreType.DMA((6,)),
        ],
        compiler_params=pltpu.CompilerParams(vmem_limit_bytes=62 << 20),
        name="outer_step",
    )(grad, shares, global_params, momentum)


def on_device(
    block_input, ssd_input, out_grad, start_state, step_bias, decay_log,
    local_params, global_params, momentum,
):
    grad, shares = step(
        block_input,
        ssd_input,
        out_grad,
        start_state,
        step_bias.reshape(1, HEADS),
        decay_log.reshape(1, HEADS),
        local_params,
    )
    return outer(grad, shares, global_params, momentum)


def solution(mesh):
    placed = (
        P(("rep", "fsdp"), None),
        P(("rep", "fsdp"), None),
        P(("rep", "fsdp"), None),
        P(("rep", "fsdp"), None, None),
        P(),
        P(),
        P("rep", "fsdp", None),
        P("fsdp", None),
        P("fsdp", None),
    )
    return jax.shard_map(
        on_device,
        mesh=mesh,
        in_specs=placed,
        out_specs=(P(("rep", "fsdp"), None), P("fsdp", None), P("fsdp", None)),
        check_vma=False,
    )
```

```python
import jax
import jax.numpy as jnp
from jax import lax
from jax.experimental import pallas as pl
from jax.experimental.pallas import tpu as pltpu
from jax.sharding import PartitionSpec as P

HEADS = 64
STATE = 64
BLOCK = 128
D = 4096
COLS = 192
NX, NYL, NYH, NZ, NC = 4, 2, 4, 12, 2
SLICE = D // (NX * NC)
HALF = D // NC
CHUNKS = 4
CHUNK = HALF // CHUNKS
STAGES = 3

inner_rate = 0.002
outer_rate = 0.7
momentum_decay = 0.9

MESH = pl.DeviceIdType.MESH
F32 = jnp.float32
BF16 = jnp.bfloat16
EXACT = lax.Precision.HIGHEST


def place():
    rep = lax.axis_index("rep")
    fsdp = lax.axis_index("fsdp")
    x = lax.rem(rep, NX)
    yl = lax.div(rep, NX)
    z = lax.div(fsdp, NYH * NC)
    yh = lax.rem(lax.div(fsdp, NC), NYH)
    c = lax.rem(fsdp, NC)
    return x, yl, yh, z, c


def device(x, yl, yh, z, c):
    return (yl * NX + x, z * (NYH * NC) + yh * NC + c)


def shift(i, by, n):
    return lax.rem(i + by, n)


def replica_group(x, yl, yh, z, c):
    return [
        device(shift(x, dx, NX), shift(yl, dy, NYL), yh, z, shift(c, dc, NC))
        for dx in range(NX)
        for dy in range(NYL)
        for dc in range(NC)
        if (dx, dy, dc) != (0, 0, 0)
    ]


def remote(src, dst, send_sem, recv_sem, target):
    return pltpu.make_async_remote_copy(
        src_ref=src,
        dst_ref=dst,
        send_sem=send_sem,
        recv_sem=recv_sem,
        device_id=target,
        device_id_type=MESH,
    )


def wait_bytes(ref, sem):
    pltpu.make_async_copy(ref, ref, sem).wait()


def dot(a, b, dims, precision=None):
    return lax.dot_general(
        a, b, ((dims[0], dims[1]), ((), ())), precision=precision, preferred_element_type=F32
    )


NN = ((1,), (0,))
NT = ((1,), (1,))
TN = ((0,), (0,))
GROUP = 8
ROWS = 128
BY_LANES = (2, 6)
LOG2E = 1.4426950408889634

PAIRS = HEADS // 2
EARLY = PAIRS - 2 * CHUNKS * STAGES


def step_kernel(
    input_hbm, values_hbm, cot_hbm, state_hbm, bias_hbm, decay_hbm, rows_hbm,
    out_hbm, shares,
    bias_ref, decay_ref, out_ref,
    input_ref, values_ref, cot_ref, state_ref, state32, rows32, rows16, shards, block32,
    w_ref, cols_ref, params_ref, inner_ref, enter_ref,
    cum_groups, row_groups, both_t, col_t, ds_ref, dq_ref, scores_ref, query_ref, pick_ref,
    mine, grads, partial, from_z, to_y, from_y, share,
    sem_load, sem_send, sem_recv, sem_x, ring_right, ring_left, sem_self,
):
    x, yl, yh, z, c = place()
    y = yh * NYL + yl
    me_a = yh * NC + c
    me_q = x * NC + c
    me_r = yl * NX + x
    own = yl == c

    def at_y(i):
        return lax.rem(i, NYL), lax.div(i, NYL)

    def half(core):
        return pl.ds(pl.multiple_of(core * HALF, HALF), HALF)

    def part(q):
        return pl.ds(pl.multiple_of(q * SLICE, SLICE), SLICE)

    def tokens(q):
        return pl.ds(pl.multiple_of(q * BLOCK, BLOCK), BLOCK)

    def rows_of(b):
        return pl.ds(pl.multiple_of(b * 16, 16), 16)

    loads = [
        pltpu.make_async_copy(src, dst, sem_load.at[i])
        for i, (src, dst) in enumerate(
            [
                (rows_hbm.at[0], rows32),
                (state_hbm.at[0], state_ref),
                (cot_hbm, cot_ref),
                (values_hbm, values_ref),
                (input_hbm, input_ref),
                (bias_hbm, bias_ref),
                (decay_hbm, decay_ref),
            ]
        )
    ]
    for load in loads:
        load.start()

    right = device(x, yl, yh, shift(z, 1, NZ), c)
    left = device(x, yl, yh, shift(z, NZ - 1, NZ), c)
    right2 = device(x, yl, yh, shift(z, 2, NZ), c)
    left2 = device(x, yl, yh, shift(z, NZ - 2, NZ), c)
    partner = device(x, yl, yh, z, 1 - c)
    along_z = [device(x, yl, yh, shift(z, dz, NZ), c) for dz in range(1, NZ)]
    along_y = []
    for dy in range(1, NYL * NYH):
        tyl, tyh = at_y(shift(y, dy, NYL * NYH))
        along_y.append(device(x, tyl, tyh, z, c))
    across = [device(x, yl, shift(yh, dy, NYH), z, 1 - c) for dy in range(1, NYH)]
    greeted = along_z + along_y + across + replica_group(x, yl, yh, z, c)
    barrier = pltpu.get_barrier_semaphore()
    for target in greeted:
        pl.semaphore_signal(barrier, inc=1, device_id=target, device_id_type=MESH)
    loads[0].wait()
    rows16[...] = rows32[...].astype(BF16)
    pl.semaphore_wait(barrier, len(greeted))

    for dy in (2, 1, 3, 0):
        for dc in range(NC):
            core = shift(c, dc, NC)
            src = rows16.at[:, half(core)]
            dst = shards.at[me_a]
            if (dy, dc) == (0, 0):
                pltpu.make_async_copy(src, dst, sem_recv.at[0]).start()
            else:
                remote(
                    src, dst, sem_send.at[0], sem_recv.at[0],
                    device(x, yl, shift(yh, dy, NYH), z, core),
                ).start()
    for dx in (2, 1, 3, 0):
        for dc in range(NC):
            tx, core = shift(x, dx, NX), shift(c, dc, NC)
            src = input_hbm.at[:, part(tx * NC + core)]
            dst = cols_ref.at[tokens(me_q)]
            if (dx, dc) == (0, 0):
                pltpu.make_async_copy(src, dst, sem_recv.at[1]).start()
            else:
                remote(
                    src, dst, sem_send.at[1], sem_recv.at[1], device(tx, yl, yh, z, core)
                ).start()
    for dx in (2, 1, 3, 0):
        for dc in range(NC):
            tx, core = shift(x, dx, NX), shift(c, dc, NC)
            src = rows32.at[:, part(tx * NC + core)]
            dst = params_ref.at[me_r]
            if (dx, dc) == (0, 0):
                pl.when(own)(pltpu.make_async_copy(src, dst, sem_recv.at[2]).start)
                copy = remote(
                    src, dst, sem_self.at[0], sem_recv.at[2], device(tx, 1 - yl, yh, z, core)
                )
                pl.when(jnp.logical_not(own))(copy.start)
            else:
                remote(
                    src, dst, sem_send.at[2], sem_recv.at[2], device(tx, c, yh, z, core)
                ).start()

    t_index = lax.broadcasted_iota(jnp.int32, (BLOCK, BLOCK), 0)
    s_index = lax.broadcasted_iota(jnp.int32, (BLOCK, BLOCK), 1)
    first = s_index < STATE
    column = lax.rem(s_index, STATE)
    origin = (s_index - column) + 2 * lax.rem(column, STATE // 2) + lax.div(column, STATE // 2)
    order = jnp.where(t_index == origin, 1.0, 0.0).astype(BF16)
    low = lax.broadcasted_iota(jnp.int32, (STATE // 2, BLOCK), 1) < STATE
    zero_state = jnp.zeros((STATE // 2, BLOCK), BF16)

    def products(p):
        lanes = tokens(p)
        cot = cot_ref[:, lanes]
        val = values_ref[:, lanes]
        zero = jnp.zeros_like(val)
        pair = jnp.concatenate(
            [jnp.where(first, val, zero), jnp.where(first, zero, val)], axis=0
        )
        inner_ref[p] = dot(cot, pair, NT)
        sorted_cot = dot(cot, order, NN).astype(BF16)
        states = []
        for e in range(2):
            st = state32[pl.ds(2 * p + e, STATE // 2, stride=HEADS), :].astype(BF16)
            kept = [jnp.where(low, st, zero_state), jnp.where(low, zero_state, st)]
            rest = [zero_state, zero_state]
            states.append(jnp.concatenate(kept + rest if e == 0 else rest + kept, axis=0))
        enter_ref[p] = dot(sorted_cot, jnp.concatenate(states, axis=1), NN)

    for load in loads[1:]:
        load.wait()
    for j in range(STATE // 2):
        state32[j * HEADS : (j + 1) * HEADS, :] = state_ref[:, j * BLOCK : (j + 1) * BLOCK].astype(F32)
    for p in range(PAIRS - EARLY, PAIRS):
        products(p)
    wait_bytes(shards, sem_recv.at[0])
    for i in range(NYH * NC):
        block32[2 * i : 2 * i + 2, :] = shards[i].astype(F32)
    w_ref[rows_of(z), half(c)] = block32[...].astype(BF16)

    def chunk(b, k):
        return w_ref.at[rows_of(b), pl.ds(pl.multiple_of(c * HALF + k * CHUNK, CHUNK), CHUNK)]

    def pass_on(b):
        block = w_ref.at[rows_of(b), half(c)]
        remote(block, block, sem_send.at[4], sem_recv.at[3], partner).start()

    def hop(b, k, sem, target):
        piece = chunk(b, k)
        return remote(piece, piece, sem_send.at[3], sem, target)

    @pl.loop(0, STAGES)
    def _(s):
        br = lax.rem(z + NZ - 2 * s, NZ)
        bl = lax.rem(z + 2 * s, NZ)
        for k in range(CHUNKS):
            pl.when(s > 0)(hop(br, k, ring_right.at[2 * s, k], right).wait_recv)
            if k < CHUNKS // 2:
                hop(br, k, ring_right.at[2 * s + 2, k], right2).start()
            else:
                pl.when(s < STAGES - 1)(hop(br, k, ring_right.at[2 * s + 2, k], right2).start)
            hop(br, k, ring_right.at[2 * s + 1, k], right).start()
            pl.when(s > 0)(hop(bl, k, ring_left.at[2 * s, k], left).wait_recv)
            if k >= CHUNKS // 2:
                hop(bl, k, ring_left.at[2 * s + 2, k], left2).start()
            else:
                pl.when(s < STAGES - 1)(hop(bl, k, ring_left.at[2 * s + 2, k], left2).start)
            hop(bl, k, ring_left.at[2 * s + 1, k], left).start()

        pass_on(br)

        @pl.when(s > 0)
        def _():
            pass_on(bl)
            fr = lax.rem(z + NZ + 1 - 2 * s, NZ)
            fl = lax.rem(z + 2 * s - 1, NZ)
            for k in range(CHUNKS):
                hop(fr, k, ring_right.at[2 * s - 1, k], right).wait_recv()
            pass_on(fr)
            for k in range(CHUNKS):
                hop(fl, k, ring_left.at[2 * s - 1, k], left).wait_recv()
            pass_on(fl)

        for i in range(2 * CHUNKS):
            products(s * 2 * CHUNKS + i)

    last = 2 * STAGES - 1
    fr, fl, far = shift(z, NZ - last, NZ), shift(z, last, NZ), shift(z, NZ // 2, NZ)
    for k in range(CHUNKS):
        hop(fr, k, ring_right.at[last, k], right).wait_recv()
    pass_on(fr)
    for k in range(CHUNKS):
        hop(fl, k, ring_left.at[last, k], left).wait_recv()
    pass_on(fl)
    for k in range(CHUNKS):
        ring = ring_right if k < CHUNKS // 2 else ring_left
        hop(far, k, ring.at[last + 1, k], right).wait_recv()
    pass_on(far)
    proj = dot(input_ref[:, half(c)], w_ref[:, half(c)], NT)
    wait_bytes(w_ref.at[:, half(1 - c)], sem_recv.at[3])
    proj = proj + dot(input_ref[:, half(1 - c)], w_ref[:, half(1 - c)], NT)
    key = proj[:, :STATE]
    query = proj[:, STATE : 2 * STATE]
    raw = proj[:, 2 * STATE :] + bias_ref[...]
    rate = jnp.exp(decay_ref[...])
    step = jnp.maximum(raw, 0.0) + jnp.log1p(jnp.exp(-jnp.abs(raw)))
    causal = t_index >= s_index
    lower = jnp.where(causal, 1.0, 0.0)
    upper = jnp.where(t_index <= s_index, 1.0, 0.0)
    cum = dot(lower, -step * rate, NN, EXACT)
    wide = jnp.concatenate([cum * LOG2E, step], axis=1)
    both_t[...] = wide.T
    for g in range(HEADS // GROUP):
        cum_groups[g] = pltpu.roll(wide, (BLOCK - GROUP * g) % BLOCK, 1) if g else wide
    scores_ref[...] = jnp.where(causal, dot(query, key, NT, EXACT), 0.0)
    query_ref[...] = jnp.concatenate([query, query], axis=1)
    by_product = [h for h in range(GROUP) if h not in BY_LANES for _ in range(2)]
    for i, h in enumerate(by_product):
        pick_ref[i * BLOCK : (i + 1) * BLOCK, :] = jnp.where(s_index == h, 1.0, 0.0).astype(BF16)
    lane_index = lax.broadcasted_iota(jnp.int32, (ROWS, BLOCK), 1)
    ds_ref[...] = jnp.zeros_like(ds_ref)
    dq_ref[...] = jnp.zeros_like(dq_ref)

    @pl.loop(0, HEADS // GROUP)
    def _(g):
        at = pl.multiple_of(g * GROUP, GROUP)
        cum_rows = both_t[pl.ds(at, GROUP), :]
        step_rows = both_t[pl.ds(HEADS + at, GROUP), :]
        cols = [jnp.zeros((8, BLOCK), F32) for _ in range(GROUP)]
        for r in range(0, BLOCK, ROWS):
            block = slice(r, r + ROWS)
            cum_g = cum_groups[g, block, :]
            score = scores_ref[block, :]
            twice = query_ref[block, :]
            ds = ds_ref[block, :]
            dq = dq_ref[block, :]
            rows = jnp.zeros((ROWS, BLOCK), F32)
            terms = []
            for h in range(GROUP):
                p = g * (GROUP // 2) + h // 2
                lanes = slice((h % 2) * BLOCK, (h % 2 + 1) * BLOCK)
                cum_t = jnp.broadcast_to(cum_g[:, h : h + 1], (ROWS, BLOCK))
                decay = jnp.exp2(jnp.minimum(cum_t - cum_rows[h : h + 1, :], 0.0))
                a = decay * inner_ref[p, block, lanes]
                step_s = step_rows[h : h + 1, :]
                ds = ds + a * step_s
                b = score * a
                cols[h] = cols[h] + jnp.sum(b.reshape(ROWS // 8, 8, BLOCK), axis=0)
                w = enter_ref[p, block, lanes] * jnp.exp2(cum_t)
                dq = dq + w
                term = b * step_s + w * twice
                if h in BY_LANES:
                    total = jnp.sum(term, axis=1, keepdims=True)
                    rows = jnp.where(lane_index == h, total, rows)
                else:
                    high = term.astype(BF16)
                    terms += [high, (term - high.astype(F32)).astype(BF16)]
            ds_ref[block, :] = ds
            dq_ref[block, :] = dq
            row_groups[g, block, :] = rows + dot(
                jnp.concatenate(terms, axis=1), pick_ref[...], NN
            )
        col_t[pl.ds(at, GROUP), :] = jnp.concatenate(
            [jnp.sum(part_sum, axis=0, keepdims=True) for part_sum in cols], axis=0
        )

    dcum = row_groups[0]
    for g in range(1, HEADS // GROUP):
        dcum = dcum + pltpu.roll(row_groups[g], GROUP * g, 1)
    dstep = col_t[...].T[:, :HEADS]
    dcum = dcum[:, :HEADS] - step * dstep
    dstep = dstep - rate * dot(upper, dcum, NN, EXACT)
    draw = dstep * jax.nn.sigmoid(raw)
    dscores = jnp.where(causal, ds_ref[...], 0.0)
    dquery = dot(dscores, key, NN, EXACT) + dq_ref[:, :STATE] + dq_ref[:, STATE:]
    dkey = dot(dscores.T, query, NN, EXACT)
    keys = jnp.concatenate([dkey, dquery], axis=1)
    steps = jnp.concatenate([draw, jnp.zeros_like(draw)], axis=1)
    mine[: 2 * STATE, :] = keys.T.astype(BF16)
    mine[2 * STATE :, :] = steps.T[:HEADS, :].astype(BF16)

    here = grads.at[:, tokens(me_q)]
    for dx in (2, 1, 3):
        remote(
            mine, here, sem_send.at[5], sem_x.at[dx], device(shift(x, dx, NX), yl, yh, z, c)
        ).start()
    remote(mine, here, sem_send.at[9], sem_recv.at[4], partner).start()
    pltpu.make_async_copy(mine, here, sem_x.at[0]).start()

    keys16 = keys.astype(BF16)
    steps16 = draw.astype(BF16)

    @pl.loop(0, D // 512)
    def _(i):
        lanes = pl.ds(pl.multiple_of(i * 512, 512), 512)
        product = dot(keys16, w_ref[: 2 * STATE, lanes], NN)
        product += dot(steps16, w_ref[2 * STATE :, lanes], NN)
        out_ref[:, lanes] = product.astype(BF16)
        pltpu.make_async_copy(out_ref.at[:, lanes], out_hbm.at[:, lanes], sem_load.at[7]).start()

    for dx in (1, 3, 2):
        there = grads.at[:, tokens(shift(x, NX - dx, NX) * NC + c)]
        copy = remote(there, there, sem_send.at[9], sem_x.at[dx], partner)
        copy.wait_recv()
        remote(there, there, sem_send.at[9], sem_recv.at[4], partner).start()
    wait_bytes(here, sem_x.at[0])
    wait_bytes(cols_ref, sem_recv.at[1])
    wait_bytes(params_ref, sem_recv.at[2])
    held = params_ref[0]
    for r in range(1, NX * NYL):
        held = held + params_ref[r]
    wait_bytes(grads.at[:, : NX * BLOCK], sem_recv.at[4])

    gradient = dot(grads[...], cols_ref[...], NN)
    for b in range(NZ):
        partial[b] = gradient[16 * b : 16 * b + 16, :].astype(BF16)
    for dz in (6, 5, 7, 4, 8, 3, 9, 2, 10, 1, 11):
        tz = shift(z, dz, NZ)
        remote(
            partial.at[tz], from_z.at[z], sem_send.at[6], sem_recv.at[5],
            device(x, yl, yh, tz, c),
        ).start()
    pltpu.make_async_copy(partial.at[z], from_z.at[z], sem_recv.at[5]).start()
    wait_bytes(from_z, sem_recv.at[5])
    total = from_z[0].astype(F32)
    for b in range(1, NZ):
        total = total + from_z[b].astype(F32)
    for i in range(NYL * NYH):
        to_y[i] = total[2 * i : 2 * i + 2, :]
    for dy in (4, 3, 5, 2, 6, 1, 7):
        ty = shift(y, dy, NYL * NYH)
        tyl, tyh = at_y(ty)
        remote(
            to_y.at[ty], from_y.at[y], sem_send.at[7], sem_recv.at[6],
            device(x, tyl, tyh, z, c),
        ).start()
    pltpu.make_async_copy(to_y.at[y], from_y.at[y], sem_recv.at[6]).start()
    wait_bytes(from_y, sem_recv.at[6])
    summed = from_y[0]
    for i in range(1, NYL * NYH):
        summed = summed + from_y[i]
    share[...] = (inner_rate * summed - held) * (1.0 / (NX * NYL))
    for dx in (2, 1, 3, 0):
        for dy in range(NYL):
            tx, tyl = shift(x, dx, NX), shift(yl, dy, NYL)
            dst = shares.at[me_q]
            if (dx, dy) == (0, 0):
                pl.when(own)(pltpu.make_async_copy(share, dst, sem_recv.at[7]).start)
                copy = remote(
                    share, dst, sem_self.at[1], sem_recv.at[7], device(tx, tyl, yh, z, 1 - c)
                )
                pl.when(jnp.logical_not(own))(copy.start)
            else:
                remote(
                    share, dst, sem_send.at[8], sem_recv.at[7], device(tx, tyl, yh, z, yl)
                ).start()
    wait_bytes(shards.at[0:7], sem_send.at[0])
    wait_bytes(cols_ref.at[0 : 7 * BLOCK], sem_send.at[1])
    wait_bytes(params_ref.at[0:7], sem_send.at[2])
    wait_bytes(w_ref.at[0 : 16 * (NZ - 1), half(c)], sem_send.at[3])
    wait_bytes(w_ref.at[:, half(c)], sem_send.at[4])
    wait_bytes(grads.at[:, : 3 * BLOCK], sem_send.at[5])
    wait_bytes(grads.at[:, : NX * BLOCK], sem_send.at[9])
    wait_bytes(from_z.at[: NZ - 1], sem_send.at[6])
    wait_bytes(from_y.at[:7], sem_send.at[7])

    @pl.when(jnp.logical_not(own))
    def _():
        wait_bytes(params_ref.at[0], sem_self.at[0])
        wait_bytes(share, sem_self.at[1])

    wait_bytes(out_ref, sem_load.at[7])
    wait_bytes(shares, sem_recv.at[7])
    wait_bytes(shares.at[:7], sem_send.at[8])


def step(block_input, values, cot, state, bias, decay, rows):
    vmem = pl.BlockSpec(memory_space=pltpu.VMEM)
    hbm = pl.BlockSpec(memory_space=pl.ANY)
    square = pltpu.VMEM((BLOCK, BLOCK), F32)
    groups = pltpu.VMEM((HEADS // GROUP, BLOCK, BLOCK), F32)
    return pl.pallas_call(
        step_kernel,
        out_shape=(
            jax.ShapeDtypeStruct((BLOCK, D), BF16),
            jax.ShapeDtypeStruct((NX * NC, 2, SLICE), F32),
        ),
        in_specs=[hbm] * 7,
        out_specs=(hbm, vmem),
        scratch_shapes=[
            pltpu.VMEM((1, HEADS), F32),
            pltpu.VMEM((1, HEADS), F32),
            pltpu.VMEM((BLOCK, D), BF16),
            pltpu.VMEM((BLOCK, D), BF16),
            pltpu.VMEM((BLOCK, D), BF16),
            pltpu.VMEM((BLOCK, D), BF16),
            pltpu.VMEM((HEADS, D), BF16),
            pltpu.VMEM((HEADS * STATE // 2, BLOCK), F32),
            pltpu.VMEM((2, D), F32),
            pltpu.VMEM((2, D), BF16),
            pltpu.VMEM((NYH * NC, 2, HALF), BF16),
            pltpu.VMEM((COLS // NZ, HALF), F32),
            pltpu.VMEM((COLS, D), BF16),
            pltpu.VMEM((NX * NC * BLOCK, SLICE), BF16),
            pltpu.VMEM((NX * NYL, 2, SLICE), F32),
            pltpu.VMEM((PAIRS, BLOCK, 2 * BLOCK), F32),
            pltpu.VMEM((PAIRS, BLOCK, 2 * BLOCK), F32),
            groups,
            groups,
            square,
            pltpu.VMEM((HEADS, BLOCK), F32),
            square,
            square,
            square,
            square,
            pltpu.VMEM((2 * (GROUP - len(BY_LANES)) * BLOCK, BLOCK), BF16),
            pltpu.VMEM((COLS, BLOCK), BF16),
            pltpu.VMEM((COLS, NX * NC * BLOCK), BF16),
            pltpu.VMEM((NZ, COLS // NZ, SLICE), BF16),
            pltpu.VMEM((NZ, COLS // NZ, SLICE), BF16),
            pltpu.VMEM((NYL * NYH, 2, SLICE), F32),
            pltpu.VMEM((NYL * NYH, 2, SLICE), F32),
            pltpu.VMEM((2, SLICE), F32),
            pltpu.SemaphoreType.DMA((8,)),
            pltpu.SemaphoreType.DMA((10,)),
            pltpu.SemaphoreType.DMA((8,)),
            pltpu.SemaphoreType.DMA((NX,)),
            pltpu.SemaphoreType.DMA((2 * STAGES + 1, CHUNKS)),
            pltpu.SemaphoreType.DMA((2 * STAGES + 1, CHUNKS)),
            pltpu.SemaphoreType.DMA((2,)),
        ],
        compiler_params=pltpu.CompilerParams(
            collective_id=0, has_side_effects=True, vmem_limit_bytes=62 << 20
        ),
        name="block_step",
    )(block_input, values, cot, state, bias, decay, rows)


def outer_kernel(
    grad_hbm, shares_hbm, global_hbm, momentum_hbm,
    out_hbm, new_params_hbm, new_momentum_hbm,
    held, shares_ref, global_ref, momentum_ref, new_params_ref, new_momentum_ref, sem_in, sem_out,
):
    width = D // 4
    cuts = [slice(i * width, (i + 1) * width) for i in range(4)]
    small = [
        pltpu.make_async_copy(src, dst, sem_in.at[4 + i])
        for i, (src, dst) in enumerate(
            [(shares_hbm, shares_ref), (global_hbm, global_ref), (momentum_hbm, momentum_ref)]
        )
    ]
    takes = [
        pltpu.make_async_copy(grad_hbm.at[:, cut], held.at[:, cut], sem_in.at[i])
        for i, cut in enumerate(cuts)
    ]
    gives = [
        pltpu.make_async_copy(held.at[:, cut], out_hbm.at[:, cut], sem_out.at[i])
        for i, cut in enumerate(cuts)
    ]
    results = [
        pltpu.make_async_copy(new_params_ref, new_params_hbm, sem_out.at[4]),
        pltpu.make_async_copy(new_momentum_ref, new_momentum_hbm, sem_out.at[5]),
    ]
    for take in small + takes:
        take.start()
    for take in small:
        take.wait()
    for q in range(NX * NC):
        cols = slice(q * SLICE, (q + 1) * SLICE)
        outer = global_ref[:, cols]
        mean_pseudo = outer + shares_ref[q]
        momentum = momentum_decay * momentum_ref[:, cols] + mean_pseudo
        new_momentum_ref[:, cols] = momentum
        new_params_ref[:, cols] = outer - outer_rate * (mean_pseudo + momentum_decay * momentum)
    for result in results:
        result.start()
    for take, give in zip(takes, gives):
        take.wait()
        give.start()
    for give in gives + results:
        give.wait()


def outer(grad, shares, global_params, momentum):
    hbm = pl.BlockSpec(memory_space=pl.ANY)
    rows = pltpu.VMEM((2, D), F32)
    return pl.pallas_call(
        outer_kernel,
        out_shape=(
            jax.ShapeDtypeStruct((BLOCK, D), BF16),
            jax.ShapeDtypeStruct((2, D), F32),
            jax.ShapeDtypeStruct((2, D), F32),
        ),
        in_specs=[hbm] * 4,
        out_specs=(hbm, hbm, hbm),
        scratch_shapes=[
            pltpu.VMEM((BLOCK, D), BF16),
            pltpu.VMEM((NX * NC, 2, SLICE), F32),
            rows,
            rows,
            rows,
            rows,
            pltpu.SemaphoreType.DMA((7,)),
            pltpu.SemaphoreType.DMA((6,)),
        ],
        compiler_params=pltpu.CompilerParams(vmem_limit_bytes=62 << 20),
        name="outer_step",
    )(grad, shares, global_params, momentum)


def on_device(
    block_input, ssd_input, out_grad, start_state, step_bias, decay_log,
    local_params, global_params, momentum,
):
    grad, shares = step(
        block_input,
        ssd_input,
        out_grad,
        start_state,
        step_bias.reshape(1, HEADS),
        decay_log.reshape(1, HEADS),
        local_params,
    )
    return outer(grad, shares, global_params, momentum)


def solution(mesh):
    placed = (
        P(("rep", "fsdp"), None),
        P(("rep", "fsdp"), None),
        P(("rep", "fsdp"), None),
        P(("rep", "fsdp"), None, None),
        P(),
        P(),
        P("rep", "fsdp", None),
        P("fsdp", None),
        P("fsdp", None),
    )
    return jax.shard_map(
        on_device,
        mesh=mesh,
        in_specs=placed,
        out_specs=(P(("rep", "fsdp"), None), P("fsdp", None), P("fsdp", None)),
        check_vma=False,
    )
```

```python
import jax
import jax.numpy as jnp
from jax import lax
from jax.experimental import pallas as pl
from jax.experimental.pallas import tpu as pltpu
from jax.sharding import PartitionSpec as P

HEADS = 64
STATE = 64
BLOCK = 128
D = 4096
COLS = 192
NX, NYL, NYH, NZ, NC = 4, 2, 4, 12, 2
SLICE = D // (NX * NC)
HALF = D // NC
CHUNKS = 4
CHUNK = HALF // CHUNKS
STAGES = 3

inner_rate = 0.002
outer_rate = 0.7
momentum_decay = 0.9

MESH = pl.DeviceIdType.MESH
F32 = jnp.float32
BF16 = jnp.bfloat16
EXACT = lax.Precision.HIGHEST


def place():
    rep = lax.axis_index("rep")
    fsdp = lax.axis_index("fsdp")
    x = lax.rem(rep, NX)
    yl = lax.div(rep, NX)
    z = lax.div(fsdp, NYH * NC)
    yh = lax.rem(lax.div(fsdp, NC), NYH)
    c = lax.rem(fsdp, NC)
    return x, yl, yh, z, c


def device(x, yl, yh, z, c):
    return (yl * NX + x, z * (NYH * NC) + yh * NC + c)


def shift(i, by, n):
    return lax.rem(i + by, n)


def replica_group(x, yl, yh, z, c):
    return [
        device(shift(x, dx, NX), shift(yl, dy, NYL), yh, z, shift(c, dc, NC))
        for dx in range(NX)
        for dy in range(NYL)
        for dc in range(NC)
        if (dx, dy, dc) != (0, 0, 0)
    ]


def remote(src, dst, send_sem, recv_sem, target):
    return pltpu.make_async_remote_copy(
        src_ref=src,
        dst_ref=dst,
        send_sem=send_sem,
        recv_sem=recv_sem,
        device_id=target,
        device_id_type=MESH,
    )


def wait_bytes(ref, sem):
    pltpu.make_async_copy(ref, ref, sem).wait()


def dot(a, b, dims, precision=None):
    return lax.dot_general(
        a, b, ((dims[0], dims[1]), ((), ())), precision=precision, preferred_element_type=F32
    )


NN = ((1,), (0,))
NT = ((1,), (1,))
TN = ((0,), (0,))
GROUP = 8
ROWS = 128
BY_LANES = (2, 6)
LOG2E = 1.4426950408889634

PAIRS = HEADS // 2
EARLY = PAIRS - 2 * CHUNKS * STAGES


def step_kernel(
    input_hbm, values_hbm, cot_hbm, state_hbm, bias_hbm, decay_hbm, rows_hbm,
    out_hbm, shares,
    bias_ref, decay_ref, out_ref,
    input_ref, values_ref, cot_ref, state_ref, state32, rows32, rows16, shards, block32,
    w_ref, cols_ref, params_ref, inner_ref, enter_ref,
    cum_groups, row_groups, both_t, col_t, ds_ref, dq_ref, scores_ref, query_ref, pick_ref,
    mine, grads, partial, from_z, to_y, from_y, share,
    sem_load, sem_send, sem_recv, sem_x, ring_right, ring_left, sem_self,
):
    x, yl, yh, z, c = place()
    y = yh * NYL + yl
    me_a = yh * NC + c
    me_q = x * NC + c
    me_r = yl * NX + x
    own = yl == c

    def at_y(i):
        return lax.rem(i, NYL), lax.div(i, NYL)

    def half(core):
        return pl.ds(pl.multiple_of(core * HALF, HALF), HALF)

    def part(q):
        return pl.ds(pl.multiple_of(q * SLICE, SLICE), SLICE)

    def tokens(q):
        return pl.ds(pl.multiple_of(q * BLOCK, BLOCK), BLOCK)

    def rows_of(b):
        return pl.ds(pl.multiple_of(b * 16, 16), 16)

    loads = [
        pltpu.make_async_copy(src, dst, sem_load.at[i])
        for i, (src, dst) in enumerate(
            [
                (rows_hbm.at[0], rows32),
                (state_hbm.at[0], state_ref),
                (cot_hbm, cot_ref),
                (values_hbm, values_ref),
                (input_hbm, input_ref),
                (bias_hbm, bias_ref),
                (decay_hbm, decay_ref),
            ]
        )
    ]
    for load in loads:
        load.start()

    right = device(x, yl, yh, shift(z, 1, NZ), c)
    left = device(x, yl, yh, shift(z, NZ - 1, NZ), c)
    right2 = device(x, yl, yh, shift(z, 2, NZ), c)
    left2 = device(x, yl, yh, shift(z, NZ - 2, NZ), c)
    partner = device(x, yl, yh, z, 1 - c)
    along_y = []
    for dy in range(1, NYL * NYH):
        tyl, tyh = at_y(shift(y, dy, NYL * NYH))
        along_y.append(device(x, tyl, tyh, z, c))
    across = [device(x, yl, shift(yh, dy, NYH), z, 1 - c) for dy in range(1, NYH)]
    greeted = [right, right2, left, left2] + along_y + across + replica_group(x, yl, yh, z, c)
    barrier = pltpu.get_barrier_semaphore()
    for target in greeted:
        pl.semaphore_signal(barrier, inc=1, device_id=target, device_id_type=MESH)
    loads[0].wait()
    rows16[...] = rows32[...].astype(BF16)
    pl.semaphore_wait(barrier, len(greeted))

    for dy in (2, 1, 3, 0):
        for dc in range(NC):
            core = shift(c, dc, NC)
            src = rows16.at[:, half(core)]
            dst = shards.at[me_a]
            if (dy, dc) == (0, 0):
                pltpu.make_async_copy(src, dst, sem_recv.at[0]).start()
            else:
                remote(
                    src, dst, sem_send.at[0], sem_recv.at[0],
                    device(x, yl, shift(yh, dy, NYH), z, core),
                ).start()
    for dx in (2, 1, 3, 0):
        for dc in range(NC):
            tx, core = shift(x, dx, NX), shift(c, dc, NC)
            src = input_hbm.at[:, part(tx * NC + core)]
            dst = cols_ref.at[tokens(me_q)]
            if (dx, dc) == (0, 0):
                pltpu.make_async_copy(src, dst, sem_recv.at[1]).start()
            else:
                remote(
                    src, dst, sem_send.at[1], sem_recv.at[1], device(tx, yl, yh, z, core)
                ).start()
    for dx in (2, 1, 3, 0):
        for dc in range(NC):
            tx, core = shift(x, dx, NX), shift(c, dc, NC)
            src = rows32.at[:, part(tx * NC + core)]
            dst = params_ref.at[me_r]
            if (dx, dc) == (0, 0):
                pl.when(own)(pltpu.make_async_copy(src, dst, sem_recv.at[2]).start)
                copy = remote(
                    src, dst, sem_self.at[0], sem_recv.at[2], device(tx, 1 - yl, yh, z, core)
                )
                pl.when(jnp.logical_not(own))(copy.start)
            else:
                remote(
                    src, dst, sem_send.at[2], sem_recv.at[2], device(tx, c, yh, z, core)
                ).start()

    t_index = lax.broadcasted_iota(jnp.int32, (BLOCK, BLOCK), 0)
    s_index = lax.broadcasted_iota(jnp.int32, (BLOCK, BLOCK), 1)
    first = s_index < STATE
    column = lax.rem(s_index, STATE)
    origin = (s_index - column) + 2 * lax.rem(column, STATE // 2) + lax.div(column, STATE // 2)
    order = jnp.where(t_index == origin, 1.0, 0.0).astype(BF16)
    low = lax.broadcasted_iota(jnp.int32, (STATE // 2, BLOCK), 1) < STATE
    zero_state = jnp.zeros((STATE // 2, BLOCK), BF16)

    def products(p):
        lanes = tokens(p)
        cot = cot_ref[:, lanes]
        val = values_ref[:, lanes]
        zero = jnp.zeros_like(val)
        pair = jnp.concatenate(
            [jnp.where(first, val, zero), jnp.where(first, zero, val)], axis=0
        )
        inner_ref[p] = dot(cot, pair, NT)
        sorted_cot = dot(cot, order, NN).astype(BF16)
        states = []
        for e in range(2):
            st = state32[pl.ds(2 * p + e, STATE // 2, stride=HEADS), :].astype(BF16)
            kept = [jnp.where(low, st, zero_state), jnp.where(low, zero_state, st)]
            rest = [zero_state, zero_state]
            states.append(jnp.concatenate(kept + rest if e == 0 else rest + kept, axis=0))
        enter_ref[p] = dot(sorted_cot, jnp.concatenate(states, axis=1), NN)

    for load in loads[1:]:
        load.wait()
    for j in range(STATE // 2):
        state32[j * HEADS : (j + 1) * HEADS, :] = state_ref[:, j * BLOCK : (j + 1) * BLOCK].astype(F32)
    for p in range(PAIRS - EARLY, PAIRS):
        products(p)
    wait_bytes(shards, sem_recv.at[0])
    for i in range(NYH * NC):
        block32[2 * i : 2 * i + 2, :] = shards[i].astype(F32)
    w_ref[rows_of(z), half(c)] = block32[...].astype(BF16)

    def chunk(b, k):
        return w_ref.at[rows_of(b), pl.ds(pl.multiple_of(c * HALF + k * CHUNK, CHUNK), CHUNK)]

    def pass_on(b):
        block = w_ref.at[rows_of(b), half(c)]
        remote(block, block, sem_send.at[4], sem_recv.at[3], partner).start()

    def hop(b, k, sem, target):
        piece = chunk(b, k)
        return remote(piece, piece, sem_send.at[3], sem, target)

    @pl.loop(0, STAGES)
    def _(s):
        br = lax.rem(z + NZ - 2 * s, NZ)
        bl = lax.rem(z + 2 * s, NZ)
        for k in range(CHUNKS):
            pl.when(s > 0)(hop(br, k, ring_right.at[2 * s, k], right).wait_recv)
            if k < CHUNKS // 2:
                hop(br, k, ring_right.at[2 * s + 2, k], right2).start()
            else:
                pl.when(s < STAGES - 1)(hop(br, k, ring_right.at[2 * s + 2, k], right2).start)
            hop(br, k, ring_right.at[2 * s + 1, k], right).start()
            pl.when(s > 0)(hop(bl, k, ring_left.at[2 * s, k], left).wait_recv)
            if k >= CHUNKS // 2:
                hop(bl, k, ring_left.at[2 * s + 2, k], left2).start()
            else:
                pl.when(s < STAGES - 1)(hop(bl, k, ring_left.at[2 * s + 2, k], left2).start)
            hop(bl, k, ring_left.at[2 * s + 1, k], left).start()

        pass_on(br)

        @pl.when(s > 0)
        def _():
            pass_on(bl)
            fr = lax.rem(z + NZ + 1 - 2 * s, NZ)
            fl = lax.rem(z + 2 * s - 1, NZ)
            for k in range(CHUNKS):
                hop(fr, k, ring_right.at[2 * s - 1, k], right).wait_recv()
            pass_on(fr)
            for k in range(CHUNKS):
                hop(fl, k, ring_left.at[2 * s - 1, k], left).wait_recv()
            pass_on(fl)

        for i in range(2 * CHUNKS):
            products(s * 2 * CHUNKS + i)

    last = 2 * STAGES - 1
    fr, fl, far = shift(z, NZ - last, NZ), shift(z, last, NZ), shift(z, NZ // 2, NZ)
    for k in range(CHUNKS):
        hop(fr, k, ring_right.at[last, k], right).wait_recv()
    pass_on(fr)
    for k in range(CHUNKS):
        hop(fl, k, ring_left.at[last, k], left).wait_recv()
    pass_on(fl)
    for k in range(CHUNKS):
        ring = ring_right if k < CHUNKS // 2 else ring_left
        hop(far, k, ring.at[last + 1, k], right).wait_recv()
    pass_on(far)
    proj = dot(input_ref[:, half(c)], w_ref[:, half(c)], NT)
    wait_bytes(w_ref.at[:, half(1 - c)], sem_recv.at[3])
    proj = proj + dot(input_ref[:, half(1 - c)], w_ref[:, half(1 - c)], NT)
    key = proj[:, :STATE]
    query = proj[:, STATE : 2 * STATE]
    raw = proj[:, 2 * STATE :] + bias_ref[...]
    rate = jnp.exp(decay_ref[...])
    step = jnp.maximum(raw, 0.0) + jnp.log1p(jnp.exp(-jnp.abs(raw)))
    causal = t_index >= s_index
    lower = jnp.where(causal, 1.0, 0.0)
    upper = jnp.where(t_index <= s_index, 1.0, 0.0)
    cum = dot(lower, -step * rate, NN, EXACT)
    wide = jnp.concatenate([cum * LOG2E, step], axis=1)
    both_t[...] = wide.T
    for g in range(HEADS // GROUP):
        cum_groups[g] = pltpu.roll(wide, (BLOCK - GROUP * g) % BLOCK, 1) if g else wide
    scores_ref[...] = jnp.where(causal, dot(query, key, NT, EXACT), 0.0)
    query_ref[...] = jnp.concatenate([query, query], axis=1)
    by_product = [h for h in range(GROUP) if h not in BY_LANES for _ in range(2)]
    for i, h in enumerate(by_product):
        pick_ref[i * BLOCK : (i + 1) * BLOCK, :] = jnp.where(s_index == h, 1.0, 0.0).astype(BF16)
    lane_index = lax.broadcasted_iota(jnp.int32, (ROWS, BLOCK), 1)
    ds_ref[...] = jnp.zeros_like(ds_ref)
    dq_ref[...] = jnp.zeros_like(dq_ref)

    @pl.loop(0, HEADS // GROUP)
    def _(g):
        at = pl.multiple_of(g * GROUP, GROUP)
        cum_rows = both_t[pl.ds(at, GROUP), :]
        step_rows = both_t[pl.ds(HEADS + at, GROUP), :]
        cols = [jnp.zeros((8, BLOCK), F32) for _ in range(GROUP)]
        for r in range(0, BLOCK, ROWS):
            block = slice(r, r + ROWS)
            cum_g = cum_groups[g, block, :]
            score = scores_ref[block, :]
            twice = query_ref[block, :]
            ds = ds_ref[block, :]
            dq = dq_ref[block, :]
            rows = jnp.zeros((ROWS, BLOCK), F32)
            terms = []
            for h in range(GROUP):
                p = g * (GROUP // 2) + h // 2
                lanes = slice((h % 2) * BLOCK, (h % 2 + 1) * BLOCK)
                cum_t = jnp.broadcast_to(cum_g[:, h : h + 1], (ROWS, BLOCK))
                decay = jnp.exp2(jnp.minimum(cum_t - cum_rows[h : h + 1, :], 0.0))
                a = decay * inner_ref[p, block, lanes]
                step_s = step_rows[h : h + 1, :]
                ds = ds + a * step_s
                b = score * a
                cols[h] = cols[h] + jnp.sum(b.reshape(ROWS // 8, 8, BLOCK), axis=0)
                w = enter_ref[p, block, lanes] * jnp.exp2(cum_t)
                dq = dq + w
                term = b * step_s + w * twice
                if h in BY_LANES:
                    total = jnp.sum(term, axis=1, keepdims=True)
                    rows = jnp.where(lane_index == h, total, rows)
                else:
                    high = term.astype(BF16)
                    terms += [high, (term - high.astype(F32)).astype(BF16)]
            ds_ref[block, :] = ds
            dq_ref[block, :] = dq
            row_groups[g, block, :] = rows + dot(
                jnp.concatenate(terms, axis=1), pick_ref[...], NN
            )
        col_t[pl.ds(at, GROUP), :] = jnp.concatenate(
            [jnp.sum(part_sum, axis=0, keepdims=True) for part_sum in cols], axis=0
        )

    dcum = row_groups[0]
    for g in range(1, HEADS // GROUP):
        dcum = dcum + pltpu.roll(row_groups[g], GROUP * g, 1)
    dstep = col_t[...].T[:, :HEADS]
    dcum = dcum[:, :HEADS] - step * dstep
    dstep = dstep - rate * dot(upper, dcum, NN, EXACT)
    draw = dstep * jax.nn.sigmoid(raw)
    dscores = jnp.where(causal, ds_ref[...], 0.0)
    dquery = dot(dscores, key, NN, EXACT) + dq_ref[:, :STATE] + dq_ref[:, STATE:]
    dkey = dot(dscores.T, query, NN, EXACT)
    keys = jnp.concatenate([dkey, dquery], axis=1)
    steps = jnp.concatenate([draw, jnp.zeros_like(draw)], axis=1)
    mine[: 2 * STATE, :] = keys.T.astype(BF16)
    mine[2 * STATE :, :] = steps.T[:HEADS, :].astype(BF16)

    here = grads.at[:, tokens(me_q)]
    for dx in (2, 1, 3):
        remote(
            mine, here, sem_send.at[5], sem_x.at[dx], device(shift(x, dx, NX), yl, yh, z, c)
        ).start()
    remote(mine, here, sem_send.at[9], sem_recv.at[4], partner).start()
    pltpu.make_async_copy(mine, here, sem_x.at[0]).start()

    keys16 = keys.astype(BF16)
    steps16 = draw.astype(BF16)

    @pl.loop(0, D // 512)
    def _(i):
        lanes = pl.ds(pl.multiple_of(i * 512, 512), 512)
        product = dot(keys16, w_ref[: 2 * STATE, lanes], NN)
        product += dot(steps16, w_ref[2 * STATE :, lanes], NN)
        out_ref[:, lanes] = product.astype(BF16)
        pltpu.make_async_copy(out_ref.at[:, lanes], out_hbm.at[:, lanes], sem_load.at[7]).start()

    for dx in (1, 3, 2):
        there = grads.at[:, tokens(shift(x, NX - dx, NX) * NC + c)]
        copy = remote(there, there, sem_send.at[9], sem_x.at[dx], partner)
        copy.wait_recv()
        remote(there, there, sem_send.at[9], sem_recv.at[4], partner).start()
    wait_bytes(here, sem_x.at[0])
    wait_bytes(cols_ref, sem_recv.at[1])
    wait_bytes(params_ref, sem_recv.at[2])
    held = params_ref[0]
    for r in range(1, NX * NYL):
        held = held + params_ref[r]
    wait_bytes(grads.at[:, : NX * BLOCK], sem_recv.at[4])

    gradient = dot(grads[...], cols_ref[...], NN)
    for b in range(NZ):
        partial[b] = gradient[16 * b : 16 * b + 16, :].astype(BF16)
    for dz in (6, 5, 7, 4, 8, 3, 9, 2, 10, 1, 11):
        tz = shift(z, dz, NZ)
        remote(
            partial.at[tz], from_z.at[z], sem_send.at[6], sem_recv.at[5],
            device(x, yl, yh, tz, c),
        ).start()
    pltpu.make_async_copy(partial.at[z], from_z.at[z], sem_recv.at[5]).start()
    wait_bytes(from_z, sem_recv.at[5])
    total = from_z[0].astype(F32)
    for b in range(1, NZ):
        total = total + from_z[b].astype(F32)
    for i in range(NYL * NYH):
        to_y[i] = total[2 * i : 2 * i + 2, :]
    for dy in (4, 3, 5, 2, 6, 1, 7):
        ty = shift(y, dy, NYL * NYH)
        tyl, tyh = at_y(ty)
        remote(
            to_y.at[ty], from_y.at[y], sem_send.at[7], sem_recv.at[6],
            device(x, tyl, tyh, z, c),
        ).start()
    pltpu.make_async_copy(to_y.at[y], from_y.at[y], sem_recv.at[6]).start()
    wait_bytes(from_y, sem_recv.at[6])
    summed = from_y[0]
    for i in range(1, NYL * NYH):
        summed = summed + from_y[i]
    share[...] = (inner_rate * summed - held) * (1.0 / (NX * NYL))
    for dx in (2, 1, 3, 0):
        for dy in range(NYL):
            tx, tyl = shift(x, dx, NX), shift(yl, dy, NYL)
            dst = shares.at[me_q]
            if (dx, dy) == (0, 0):
                pl.when(own)(pltpu.make_async_copy(share, dst, sem_recv.at[7]).start)
                copy = remote(
                    share, dst, sem_self.at[1], sem_recv.at[7], device(tx, tyl, yh, z, 1 - c)
                )
                pl.when(jnp.logical_not(own))(copy.start)
            else:
                remote(
                    share, dst, sem_send.at[8], sem_recv.at[7], device(tx, tyl, yh, z, yl)
                ).start()
    wait_bytes(shards.at[0:7], sem_send.at[0])
    wait_bytes(cols_ref.at[0 : 7 * BLOCK], sem_send.at[1])
    wait_bytes(params_ref.at[0:7], sem_send.at[2])
    wait_bytes(w_ref.at[0 : 16 * (NZ - 1), half(c)], sem_send.at[3])
    wait_bytes(w_ref.at[:, half(c)], sem_send.at[4])
    wait_bytes(grads.at[:, : 3 * BLOCK], sem_send.at[5])
    wait_bytes(grads.at[:, : NX * BLOCK], sem_send.at[9])
    wait_bytes(from_z.at[: NZ - 1], sem_send.at[6])
    wait_bytes(from_y.at[:7], sem_send.at[7])

    @pl.when(jnp.logical_not(own))
    def _():
        wait_bytes(params_ref.at[0], sem_self.at[0])
        wait_bytes(share, sem_self.at[1])

    wait_bytes(out_ref, sem_load.at[7])
    wait_bytes(shares, sem_recv.at[7])
    wait_bytes(shares.at[:7], sem_send.at[8])


def step(block_input, values, cot, state, bias, decay, rows):
    vmem = pl.BlockSpec(memory_space=pltpu.VMEM)
    hbm = pl.BlockSpec(memory_space=pl.ANY)
    square = pltpu.VMEM((BLOCK, BLOCK), F32)
    groups = pltpu.VMEM((HEADS // GROUP, BLOCK, BLOCK), F32)
    return pl.pallas_call(
        step_kernel,
        out_shape=(
            jax.ShapeDtypeStruct((BLOCK, D), BF16),
            jax.ShapeDtypeStruct((NX * NC, 2, SLICE), F32),
        ),
        in_specs=[hbm] * 7,
        out_specs=(hbm, vmem),
        scratch_shapes=[
            pltpu.VMEM((1, HEADS), F32),
            pltpu.VMEM((1, HEADS), F32),
            pltpu.VMEM((BLOCK, D), BF16),
            pltpu.VMEM((BLOCK, D), BF16),
            pltpu.VMEM((BLOCK, D), BF16),
            pltpu.VMEM((BLOCK, D), BF16),
            pltpu.VMEM((HEADS, D), BF16),
            pltpu.VMEM((HEADS * STATE // 2, BLOCK), F32),
            pltpu.VMEM((2, D), F32),
            pltpu.VMEM((2, D), BF16),
            pltpu.VMEM((NYH * NC, 2, HALF), BF16),
            pltpu.VMEM((COLS // NZ, HALF), F32),
            pltpu.VMEM((COLS, D), BF16),
            pltpu.VMEM((NX * NC * BLOCK, SLICE), BF16),
            pltpu.VMEM((NX * NYL, 2, SLICE), F32),
            pltpu.VMEM((PAIRS, BLOCK, 2 * BLOCK), F32),
            pltpu.VMEM((PAIRS, BLOCK, 2 * BLOCK), F32),
            groups,
            groups,
            square,
            pltpu.VMEM((HEADS, BLOCK), F32),
            square,
            square,
            square,
            square,
            pltpu.VMEM((2 * (GROUP - len(BY_LANES)) * BLOCK, BLOCK), BF16),
            pltpu.VMEM((COLS, BLOCK), BF16),
            pltpu.VMEM((COLS, NX * NC * BLOCK), BF16),
            pltpu.VMEM((NZ, COLS // NZ, SLICE), BF16),
            pltpu.VMEM((NZ, COLS // NZ, SLICE), BF16),
            pltpu.VMEM((NYL * NYH, 2, SLICE), F32),
            pltpu.VMEM((NYL * NYH, 2, SLICE), F32),
            pltpu.VMEM((2, SLICE), F32),
            pltpu.SemaphoreType.DMA((8,)),
            pltpu.SemaphoreType.DMA((10,)),
            pltpu.SemaphoreType.DMA((8,)),
            pltpu.SemaphoreType.DMA((NX,)),
            pltpu.SemaphoreType.DMA((2 * STAGES + 1, CHUNKS)),
            pltpu.SemaphoreType.DMA((2 * STAGES + 1, CHUNKS)),
            pltpu.SemaphoreType.DMA((2,)),
        ],
        compiler_params=pltpu.CompilerParams(
            collective_id=0, has_side_effects=True, vmem_limit_bytes=62 << 20
        ),
        name="block_step",
    )(block_input, values, cot, state, bias, decay, rows)


def outer_kernel(
    grad_hbm, shares_hbm, global_hbm, momentum_hbm,
    out_hbm, new_params_hbm, new_momentum_hbm,
    held, shares_ref, global_ref, momentum_ref, new_params_ref, new_momentum_ref, sem_in, sem_out,
):
    width = D // 4
    cuts = [slice(i * width, (i + 1) * width) for i in range(4)]
    small = [
        pltpu.make_async_copy(src, dst, sem_in.at[4 + i])
        for i, (src, dst) in enumerate(
            [(shares_hbm, shares_ref), (global_hbm, global_ref), (momentum_hbm, momentum_ref)]
        )
    ]
    takes = [
        pltpu.make_async_copy(grad_hbm.at[:, cut], held.at[:, cut], sem_in.at[i])
        for i, cut in enumerate(cuts)
    ]
    gives = [
        pltpu.make_async_copy(held.at[:, cut], out_hbm.at[:, cut], sem_out.at[i])
        for i, cut in enumerate(cuts)
    ]
    results = [
        pltpu.make_async_copy(new_params_ref, new_params_hbm, sem_out.at[4]),
        pltpu.make_async_copy(new_momentum_ref, new_momentum_hbm, sem_out.at[5]),
    ]
    for take in small + takes:
        take.start()
    for take in small:
        take.wait()
    for q in range(NX * NC):
        cols = slice(q * SLICE, (q + 1) * SLICE)
        outer = global_ref[:, cols]
        mean_pseudo = outer + shares_ref[q]
        momentum = momentum_decay * momentum_ref[:, cols] + mean_pseudo
        new_momentum_ref[:, cols] = momentum
        new_params_ref[:, cols] = outer - outer_rate * (mean_pseudo + momentum_decay * momentum)
    for result in results:
        result.start()
    for take, give in zip(takes, gives):
        take.wait()
        give.start()
    for give in gives + results:
        give.wait()


def outer(grad, shares, global_params, momentum):
    hbm = pl.BlockSpec(memory_space=pl.ANY)
    rows = pltpu.VMEM((2, D), F32)
    return pl.pallas_call(
        outer_kernel,
        out_shape=(
            jax.ShapeDtypeStruct((BLOCK, D), BF16),
            jax.ShapeDtypeStruct((2, D), F32),
            jax.ShapeDtypeStruct((2, D), F32),
        ),
        in_specs=[hbm] * 4,
        out_specs=(hbm, hbm, hbm),
        scratch_shapes=[
            pltpu.VMEM((BLOCK, D), BF16),
            pltpu.VMEM((NX * NC, 2, SLICE), F32),
            rows,
            rows,
            rows,
            rows,
            pltpu.SemaphoreType.DMA((7,)),
            pltpu.SemaphoreType.DMA((6,)),
        ],
        compiler_params=pltpu.CompilerParams(vmem_limit_bytes=62 << 20),
        name="outer_step",
    )(grad, shares, global_params, momentum)


def on_device(
    block_input, ssd_input, out_grad, start_state, step_bias, decay_log,
    local_params, global_params, momentum,
):
    grad, shares = step(
        block_input,
        ssd_input,
        out_grad,
        start_state,
        step_bias.reshape(1, HEADS),
        decay_log.reshape(1, HEADS),
        local_params,
    )
    return outer(grad, shares, global_params, momentum)


def solution(mesh):
    placed = (
        P(("rep", "fsdp"), None),
        P(("rep", "fsdp"), None),
        P(("rep", "fsdp"), None),
        P(("rep", "fsdp"), None, None),
        P(),
        P(),
        P("rep", "fsdp", None),
        P("fsdp", None),
        P("fsdp", None),
    )
    return jax.shard_map(
        on_device,
        mesh=mesh,
        in_specs=placed,
        out_specs=(P(("rep", "fsdp"), None), P("fsdp", None), P("fsdp", None)),
        check_vma=False,
    )
```
